128 devices in a mesh: ctx: 32 (over x, y, core), row: 4 (over z).
Axes of the slice: x: 4, y: 4, z: 4, core: 2. Of those that a mesh axis runs over, the one named last changes fastest.
Arguments:
- latent_cache: bfloat16 [131072, 576], P(('ctx', 'row')), may hold values from -8 to 8
- index_keys: bfloat16 [131072, 128], P('ctx'), may hold values from -6 to 6
- query_latent: bfloat16 [512, 128, 576], P(('row', 'ctx')), may hold values from -100 to 99
- index_query: bfloat16 [512, 64, 128], P(('row', 'ctx')), may hold values from -0.5 to 0.5
- index_gates: bfloat16 [512, 64], P(('row', 'ctx')), may hold values from -0.75 to 0.75
- selected: int32 [512, 2048], P(('row', 'ctx')), may hold values from 0 to 131071, as said below
Outputs:
- attended: bfloat16 [512, 128, 512], P(('row', 'ctx'))
- index_scores: float32 [512, 131072], P('row', 'ctx')
The draws below stay inside these ranges and needn't reach their ends.
Inputs may be any that keep to these rules, and one draw needn't show every extreme that they name: `selected`: each row names 2048 different tokens. Among the tokens of one index of ctx (s * 4096 <= t < (s + 1) * 4096) a row names at most 256, and exactly 256 in one such range; a row names at most one token in each aligned run of 16 tokens.
All inputs are finite; a program needn't handle non-finite values.
Results may differ from the reference program's by a relative error of at most 0.0045.
Values may be sent and summed in bfloat16 or wider, within the bound.
A program may use at most 256 MiB of HBM per device.

```python
import jax
import jax.numpy as jnp
from jax import lax

HEADS = 128
LATENT = 512
ROPE = 64
IHEADS = 64
IDIM = 128
TOPK = 2048
SCORE_DIM = 192
SEL_MOST = 256
TOK_DEV = 4096
CACHE = 131072
ROWS = 512


def pick_tokens(key):
    base = jax.random.fold_in(key, 11)
    key_bias, key_forced, key_noise, key_jitter = jax.random.split(base, 4)
    shards = CACHE // TOK_DEV
    slots = shards * SEL_MOST
    spacing = TOK_DEV // SEL_MOST
    bias = jax.random.randint(key_bias, (ROWS, shards), 0, shards) + jnp.arange(shards, dtype=jnp.int32)[None, :]
    forced = jax.random.randint(key_forced, (ROWS,), 0, shards)
    bias = jnp.where(jnp.arange(shards, dtype=jnp.int32)[None, :] == forced[:, None], 8 * shards, bias)
    shard_of_slot = jnp.arange(slots, dtype=jnp.int32) // SEL_MOST
    noise = jax.random.randint(key_noise, (ROWS, slots), 0, 2 * shards)
    ranking = (bias[:, shard_of_slot] + noise) * slots + jnp.arange(slots, dtype=jnp.int32)[None, :]
    chosen = lax.top_k(ranking, TOPK)[1].astype(jnp.int32)
    shard = chosen // SEL_MOST
    place = chosen % SEL_MOST
    jitter = jax.random.randint(key_jitter, (ROWS, TOPK), 0, spacing)
    return (shard * TOK_DEV + place * spacing + jitter).astype(jnp.int32)


def cache_field(key):
    base = jax.random.normal(jax.random.fold_in(key, 23), (CACHE, LATENT + ROPE), jnp.float32)
    base = jnp.clip(base, -6.0, 6.0)
    return base


def draw_latent_cache(key, part):
    return cache_field(key).astype(jnp.bfloat16)


def draw_selected(key, part):
    return pick_tokens(key)


def draw_query_latent(key, part):
    query = jnp.clip(jax.random.normal(jax.random.fold_in(key, 37), (ROWS, HEADS, LATENT + ROPE), jnp.float32), -6.0, 6.0)
    return query.astype(jnp.bfloat16)


def block_scale(own_key, shape, pieces, least, high):
    loudness = 1.0
    for axis_at, parts in pieces:
        steps = jax.random.uniform(jax.random.fold_in(jax.random.fold_in(own_key, 6), axis_at), (parts,), jnp.float32, least / len(pieces), high / len(pieces))
        loudness = loudness * jnp.repeat(jnp.exp(steps), shape[axis_at] // parts).reshape((-1,) + (1,) * (len(shape) - 1 - axis_at))
    return loudness


def gaussian(key, shape, spread, limit, cuts=(), kind=jnp.bfloat16):
    entries = jax.random.normal(key, shape, jnp.float32) * spread
    if len(cuts) > 0:
        entries = block_scale(key, shape, cuts, -0.22, 0.18) * entries
    return jnp.clip(entries, min=-limit, max=limit).astype(kind)


def setup_inputs(seed: int = 0) -> dict:
    key_list = jax.random.split(jax.random.key(seed), 7)
    latent_cache = draw_latent_cache(jax.random.fold_in(key_list[6], 71), 0)
    index_keys = gaussian(key_list[1], (CACHE, IDIM), 1.0, 6.0, ((0, 32),))
    query_latent = draw_query_latent(jax.random.fold_in(key_list[6], 71), 0)
    index_query = gaussian(key_list[3], (ROWS, IHEADS, IDIM), IDIM ** -0.5, 0.5, ((0, 128),))
    index_gates = gaussian(key_list[4], (ROWS, IHEADS), IHEADS ** -0.5, 0.75, ((0, 128),))
    selected = draw_selected(jax.random.fold_in(key_list[6], 71), 0)
    return {"latent_cache": latent_cache, "index_keys": index_keys, "query_latent": query_latent, "index_query": index_query, "index_gates": index_gates, "selected": selected}


def reference(latent_cache, index_keys, query_latent, index_query, index_gates, selected):
    scale = SCORE_DIM ** -0.5

    def attend_row(pair):
        query, picks = pair
        keys = latent_cache[picks]
        scores = jnp.dot(query, keys.T, preferred_element_type=jnp.float32) * scale
        peak = jnp.max(scores, axis=1, keepdims=True)
        weights = jnp.exp(scores - peak).astype(jnp.bfloat16)
        totals = jnp.sum(weights.astype(jnp.float32), axis=1)
        sums = jnp.dot(weights, keys[:, :LATENT], preferred_element_type=jnp.float32)
        return (sums / totals[:, None]).astype(jnp.bfloat16)

    attended = lax.map(attend_row, (query_latent, selected))

    def index_row(pair):
        iquery, gates = pair
        logits = jnp.dot(iquery, index_keys.T, preferred_element_type=jnp.float32)
        return jnp.sum(gates.astype(jnp.float32)[:, None] * jnp.maximum(logits, 0.0), axis=0)

    index_scores = lax.map(index_row, (index_query, index_gates))
    return attended, index_scores
```

```python
import jax
import jax.numpy as jnp
from jax import lax
from jax.experimental import pallas as pl
from jax.experimental.pallas import tpu as pltpu
from jax.sharding import PartitionSpec as P

MESH = pl.DeviceIdType.MESH
LATENT = 512
SCALE = 192 ** (-0.5)
NONE = -1e30
FLOOR = -1e29
F32 = jnp.float32
BF16 = jnp.bfloat16
NT = (((1,), (1,)), ((), ()))


def remote(src, dst, send, recv, device):
    return pltpu.make_async_remote_copy(
        src_ref=src, dst_ref=dst, send_sem=send, recv_sem=recv, device_id=device, device_id_type=MESH
    )


def place(core):
    chip = lax.axis_index("ctx") // 2
    x, y = chip // 4, chip % 4
    return x * (1 - core) + y * core, y * (1 - core) + x * core


def chip_of(a, b, core):
    a, b = a % 4, b % 4
    return (a * (1 - core) + b * core) * 4 + b * (1 - core) + a * core


class Ring:
    def __init__(self, own, buf, rows, send, recv, core, on_block=None):
        self.own, self.buf, self.send, self.recv, self.core = own, buf, send, recv, core
        self.halves = (pl.ds(0, rows), pl.ds(0, rows // 2), pl.ds(rows // 2, rows // 2))
        self.a, self.b = place(core)
        self.columns = (self.a, self.a + 3, self.a + 1, self.a + 2)
        self.sent = []
        self.on_block = on_block

    def view(self, a, b, part):
        return self.buf(chip_of(a, b, self.core), self.halves[part])

    def put(self, k, block, part, to, own=False):
        src = self.own if own else self.view(*block, part)
        device = {"ctx": chip_of(*to, self.core) * 2 + self.core}
        copy = remote(src, self.view(*block, part), self.send.at[k], self.recv.at[k], device)
        copy.start()
        self.sent.append(copy)

    def get(self, k, block, part, event):
        ref = self.view(*block, part)
        remote(ref, ref, self.send.at[k], self.recv.at[k], {"ctx": lax.axis_index("ctx")}).wait_recv()
        if self.on_block is not None:
            self.on_block(event, block, part)

    def start(self):
        a, b = self.a, self.b
        self.put(4, (a, b), 0, (a, b + 1), own=True)
        self.put(5, (a, b), 0, (a, b + 3), own=True)
        self.put(0, (a, b), 0, (a + 1, b), own=True)
        self.put(1, (a, b), 0, (a + 3, b), own=True)

    def second(self, j):
        block = (self.columns[j], self.b)
        self.put(4 + 4 * j, block, 0, (self.a, self.b + 1))
        self.put(5 + 4 * j, block, 0, (self.a, self.b + 3))

    def near(self):
        a, b = self.a, self.b
        self.get(0, (a + 3, b), 0, 1)
        self.put(2, (a + 3, b), 1, (a + 1, b))
        self.second(1)
        self.get(1, (a + 1, b), 0, 2)
        self.put(3, (a + 1, b), 2, (a + 3, b))
        self.second(2)

    def far(self):
        a, b = self.a, self.b
        self.get(2, (a + 2, b), 1, 3)
        self.get(3, (a + 2, b), 2, 4)
        self.second(3)

    def relay(self, j):
        column, b = self.columns[j], self.b
        self.get(4 + 4 * j, (column, b + 3), 0, 5 + 4 * j)
        self.put(6 + 4 * j, (column, b + 3), 1, (self.a, b + 1))
        self.get(5 + 4 * j, (column, b + 1), 0, 6 + 4 * j)
        self.put(7 + 4 * j, (column, b + 1), 2, (self.a, b + 3))

    def last(self, j):
        column, b = self.columns[j], self.b
        self.get(6 + 4 * j, (column, b + 2), 1, 7 + 4 * j)
        self.get(7 + 4 * j, (column, b + 2), 2, 8 + 4 * j)

    def finish(self):
        for copy in self.sent:
            copy.wait_send()


def gather_kernel(
    q_ref, k_ref, iq_ref, keys_ref, sel_ref,
    qall, kall, tall, isc_ref,
    iqall, tsend, gate_ref,
    q_send, q_recv, i_send, i_recv, p_send, p_recv, k_send, k_recv, t_send, t_recv, local,
):
    ctx, z = lax.axis_index("ctx"), lax.axis_index("row")
    core, chip = ctx % 2, ctx // 2
    other = 1 - core
    partner = {"ctx": chip * 2 + other}

    barrier = pltpu.get_barrier_semaphore()
    for step in range(1, 16):
        pl.semaphore_signal(
            barrier, inc=1, device_id={"ctx": ((chip + step) % 16) * 2 + core}, device_id_type=MESH
        )
    pl.semaphore_signal(barrier, inc=1, device_id=partner, device_id_type=MESH)
    for step in (1, 3):
        pl.semaphore_signal(barrier, inc=1, device_id={"row": (z + step) % 4}, device_id_type=MESH)

    def add_picks(i, total):
        token = sel_ref[pl.ds(i, 1), :]
        to = (token >> 13) * 16 + ((token >> 4) & 15)
        window = (i // 4) * 32 + ((token >> 8) & 31)
        value = ((token & 255) + 1).astype(F32)
        width = token.shape[1]
        left = lax.broadcasted_iota(jnp.int32, (256, width), 0) == to
        right = lax.broadcasted_iota(jnp.int32, (128, width), 0) == window
        return total + lax.dot_general(
            jnp.where(left, 1.0, 0.0).astype(BF16),
            jnp.where(right, value, 0.0).astype(BF16),
            NT,
            preferred_element_type=F32,
        )

    table = lax.fori_loop(0, sel_ref.shape[0], add_picks, jnp.zeros((256, 128), F32))
    tsend[...] = table.astype(BF16).reshape(16, 16, 128)

    pl.semaphore_wait(barrier, 18)

    to_partner = []

    def hand_on(event, block, part):
        ref = index_ring.view(*block, part)
        copy = remote(ref, ref, p_send.at[event], p_recv.at[event], partner)
        copy.start()
        to_partner.append(copy)

    index_ring = Ring(
        iq_ref, lambda p, rows: iqall.at[p, core, rows], iq_ref.shape[0], i_send, i_recv, core, hand_on
    )
    index_ring.start()
    copy = remote(iq_ref, iqall.at[chip, core], p_send.at[0], p_recv.at[0], partner)
    copy.start()
    to_partner.append(copy)

    table_copies = []
    for step in range(1, 16):
        to = (chip + step) % 16
        copy = remote(
            tsend.at[to], tall.at[chip], t_send.at[step], t_recv.at[step], {"ctx": to * 2 + core}
        )
        copy.start()
        table_copies.append(copy)

    k_rows = k_ref.shape[0]
    parts = (pl.ds(0, k_rows), pl.ds(0, k_rows // 2), pl.ds(k_rows // 2, k_rows // 2))
    k_sent = []

    def k_view(depth, part, c=core):
        return kall.at[c * 4 + depth % 4, parts[part]]

    def k_put(k, src, dst, device):
        copy = remote(src, dst, k_send.at[k], k_recv.at[k], device)
        copy.start()
        k_sent.append(copy)

    def k_get(k, depth, part, c=core):
        ref = k_view(depth, part, c)
        remote(ref, ref, k_send.at[k], k_recv.at[k], {"row": z}).wait_recv()

    up, down = {"row": (z + 1) % 4}, {"row": (z + 3) % 4}
    k_put(0, k_ref, k_view(z, 0), up)
    k_put(1, k_ref, k_view(z, 0), down)
    k_put(4, k_ref, k_view(z, 0), partner)

    query_ring = Ring(q_ref, lambda p, rows: qall.at[p, rows], q_ref.shape[0], q_send, q_recv, core)
    query_ring.start()

    own = [
        pltpu.make_async_copy(q_ref, qall.at[chip], local.at[0]),
        pltpu.make_async_copy(k_ref, k_view(z, 0), local.at[1]),
        pltpu.make_async_copy(tsend.at[chip], tall.at[chip], local.at[2]),
        pltpu.make_async_copy(iq_ref, iqall.at[chip, core], local.at[3]),
    ]
    for copy in own:
        copy.start()

    index_ring.near()
    index_ring.relay(0)
    index_ring.far()
    index_ring.relay(1)
    index_ring.relay(2)
    index_ring.last(0)
    index_ring.relay(3)
    for j in (1, 2, 3):
        index_ring.last(j)

    oa, ob = place(other)
    columns = (oa, oa + 3, oa + 1, oa + 2)
    arrivals = [(0, (oa, ob), 0), (1, (oa + 3, ob), 0), (2, (oa + 1, ob), 0), (3, (oa + 2, ob), 1), (4, (oa + 2, ob), 2)]
    for j in range(4):
        column = columns[j]
        arrivals += [
            (5 + 4 * j, (column, ob + 3), 0),
            (6 + 4 * j, (column, ob + 1), 0),
            (7 + 4 * j, (column, ob + 2), 1),
            (8 + 4 * j, (column, ob + 2), 2),
        ]
    for event, block, part in arrivals:
        ref = iqall.at[chip_of(*block, other), other, index_ring.halves[part]]
        remote(ref, ref, p_send.at[event], p_recv.at[event], partner).wait_recv()
    own[3].wait()

    tile = 512

    def index_chip(p, carry):
        for c in range(2):
            gates = iqall[p, c, 256:320, :].astype(F32)
            for r in range(4):
                gate_ref[pl.ds((c * 4 + r) * 64, 64), :] = jnp.broadcast_to(gates[:, r : r + 1], (64, 128))
        queries = iqall[p, :, 0:256, :].reshape(512, 128)

        def some_tokens(t, carry):
            at = pl.ds(pl.multiple_of(t * tile, tile), tile)
            logits = lax.dot_general(queries, keys_ref[at, :], NT, preferred_element_type=F32)
            rows = []
            for i in range(8):
                gate = jnp.concatenate([gate_ref[pl.ds(i * 64, 64), :]] * (tile // 128), axis=1)
                part = jnp.maximum(logits[i * 64 : (i + 1) * 64, :], 0.0) * gate
                rows.append(jnp.sum(part, axis=0, keepdims=True))
            isc_ref[pl.ds(pl.multiple_of(p * 8, 8), 8), at] = jnp.concatenate(rows, axis=0)
            return carry

        return lax.fori_loop(0, keys_ref.shape[0] // tile, some_tokens, carry)

    def index_chips(low, high):
        lax.fori_loop(low, high, index_chip, 0)

    index_chips(0, 2)
    query_ring.near()
    query_ring.relay(0)
    index_chips(2, 6)
    k_get(0, z + 3, 0)
    k_put(2, k_view(z + 3, 1), k_view(z + 3, 1), up)
    k_put(5, k_view(z + 3, 0), k_view(z + 3, 0), partner)
    k_get(1, z + 1, 0)
    k_put(3, k_view(z + 1, 2), k_view(z + 1, 2), down)
    k_put(6, k_view(z + 1, 0), k_view(z + 1, 0), partner)
    query_ring.far()
    index_chips(6, 9)
    query_ring.relay(1)
    query_ring.relay(2)
    index_chips(9, 13)
    k_get(2, z + 2, 1)
    k_put(7, k_view(z + 2, 1), k_view(z + 2, 1), partner)
    k_get(3, z + 2, 2)
    k_put(8, k_view(z + 2, 2), k_view(z + 2, 2), partner)
    query_ring.relay(3)
    index_chips(13, 16)

    for j in range(4):
        query_ring.last(j)
    k_get(4, z, 0, other)
    k_get(5, z + 3, 0, other)
    k_get(6, z + 1, 0, other)
    k_get(7, z + 2, 1, other)
    k_get(8, z + 2, 2, other)
    for step in range(1, 16):
        frm = (chip + 16 - step) % 16
        remote(
            tall.at[frm], tall.at[frm], t_send.at[step], t_recv.at[step], partner
        ).wait_recv()
    for copy in own[:3]:
        copy.wait()
    query_ring.finish()
    index_ring.finish()
    for copy in to_partner + table_copies + k_sent:
        copy.wait_send()


def attend_kernel(
    qall, kall, tall, out_ref,
    kext, ksel, qbuf, picks, mlcol, mlin,
    s_opp, s_up, s_dn, r_opp0, r_opp1, r_up, r_dn,
    m_opp, m_up, m_dn, n_opp0, n_opp1, n_up, n_dn,
    acc, t_opp, t_up, t_dn, w_opp0, w_opp1, w_up, w_dn,
    e_opp, e_up, e_dn, f_opp0, f_opp1, f_up, f_dn,
    k_sem, q_sem, send, recv,
):
    ctx = lax.axis_index("ctx")
    core = ctx % 2
    u, v = place(core)
    up_u = {"ctx": chip_of(u + 1, v, core) * 2 + core}
    dn_u = {"ctx": chip_of(u + 3, v, core) * 2 + core}
    up_v = {"ctx": chip_of(u, v + 1, core) * 2 + core}
    dn_v = {"ctx": chip_of(u, v + 3, core) * 2 + core}
    order = (2, 1, 3, 0)

    barrier = pltpu.get_barrier_semaphore()
    for device in (up_u, dn_u, up_v, dn_v):
        pl.semaphore_signal(barrier, inc=1, device_id=device, device_id_type=MESH)

    def k_copy(w):
        at = pl.ds(pl.multiple_of((w % 4) * 256, 256), 256)
        return pltpu.make_async_copy(kall.at[w // 4, :, at], kext.at[w, pl.ds(0, 576), :], k_sem.at[w])

    def q_copies(chunk):
        return [
            pltpu.make_async_copy(
                qall.at[chip_of(u + order[chunk], v + order[j], core)],
                qbuf.at[chunk % 2, j],
                q_sem.at[chunk % 2, j],
            )
            for j in range(4)
        ]

    def start_k(w, carry):
        k_copy(w).start()
        return carry

    lax.fori_loop(0, 32, start_k, 0)
    for copy in q_copies(0):
        copy.start()

    ones = jnp.where(lax.broadcasted_iota(jnp.int32, (64, 256), 0) == 0, 1.0, 0.0).astype(BF16)

    def set_ones(w, carry):
        kext[w, pl.ds(576, 64), :] = ones
        return carry

    lax.fori_loop(0, 32, set_ones, 0)
    pl.semaphore_wait(barrier, 4)

    sent = []

    def put(k, src, dst, device):
        copy = remote(src, dst, send.at[k], recv.at[k], device)
        copy.start()
        sent.append(copy)

    def get(k, ref):
        remote(ref, ref, send.at[k], recv.at[k], up_u).wait_recv()

    lane = lax.broadcasted_iota(jnp.int32, (128, 128), 1)

    def column(ref, at):
        return jnp.sum(jnp.where(lane == at, ref[...], 0.0), axis=1, keepdims=True)

    def keep(ref, at, peak, total):
        ref[...] = jnp.where(lane == at, peak, jnp.where(lane == at + 1, total, ref[...]))

    def flip_in(slot, ref):
        rows = ref.shape[0]
        full = jnp.concatenate([ref[...], jnp.zeros((128 - rows, 128), F32)], axis=0)
        mlin[slot] = full.T

    def joined(one, two):
        sums1, peak1, total1 = one
        sums2, peak2, total2 = two
        peak = jnp.maximum(peak1, peak2)
        f1, f2 = jnp.exp(peak1 - peak), jnp.exp(peak2 - peak)
        return sums1 * f1 + sums2.astype(F32) * f2, peak, total1 * f1 + total2 * f2

    def gather_tokens(chunk):
        for j in range(4):
            t = tall[chip_of(u + order[chunk], v + order[j], core)].astype(F32)
            for r in range(4):
                moved = t if r == 0 else pltpu.roll(t, 128 - r * 32, axis=1)
                picks[pl.ds((j * 4 + r) * 16, 16), :] = moved
        wide = lax.broadcasted_iota(jnp.int32, (256, 128), 1)
        token = (lax.broadcasted_iota(jnp.int32, (256, 256), 1) + 1).astype(F32)

        def one_window(w, carry):
            if chunk == 0:
                k_copy(w).wait()
            want = jnp.sum(jnp.where(wide == w, picks[...], 0.0), axis=1, keepdims=True)
            onehot = jnp.where(token == want, 1.0, 0.0).astype(BF16)
            rows = lax.dot_general(onehot, kext[w], NT, preferred_element_type=F32)
            at = pl.ds(pl.multiple_of(w * 16, 16), 16)
            ksel[:, at, :] = rows.astype(BF16).reshape(16, 16, 640)
            return carry

        lax.fori_loop(0, 32, one_window, 0)

    probe = jnp.where(lax.broadcasted_iota(jnp.int32, (16, 128), 1) == 64, 1.0, 0.0).astype(BF16)

    def attend_row(slot, j, r):
        row = j * 4 + r
        latent = ksel[row, :, 0:512]
        rope = qbuf[slot, j, :, 2048 + r * 64 : 2048 + (r + 1) * 64]
        rope = jnp.concatenate([rope, jnp.zeros((128, 64), BF16)], axis=1)
        rope = jnp.concatenate([rope, probe], axis=0)
        query = qbuf[slot, j, :, r * 512 : (r + 1) * 512]
        extra = lax.dot_general(rope, ksel[row, :, 512:640], NT, preferred_element_type=F32)
        scores = lax.dot_general(query, latent, NT, preferred_element_type=F32)
        scores = (scores + extra[0:128]) * SCALE
        scores = jnp.where(extra[128:129] > 0.5, scores, NONE)
        peak = jnp.maximum(jnp.max(scores, axis=1, keepdims=True), FLOOR)
        weights = jnp.exp(scores - peak).astype(BF16)
        total = jnp.sum(weights.astype(F32), axis=1, keepdims=True)
        sums = jnp.dot(weights, latent, preferred_element_type=F32)
        return sums, peak, total

    def half_chunk(chunk, half, put_row, merges):
        def one_block(j, carry):
            for r2 in range(2):
                got = attend_row(chunk % 2, j, half * 2 + r2)
                for slot, ref in merges:
                    at = j * 4 + r2 * 2
                    got = joined(got, (ref[j, r2], column(mlin.at[slot], at), column(mlin.at[slot], at + 1)))
                put_row(j, r2, *got)
            return carry

        lax.fori_loop(0, 4, one_block, 0)

    def send_half(chunk, half, sums_ref, ml_ref, merges):
        def put_row(j, r2, sums, peak, total):
            sums_ref[half, j, r2] = sums.astype(BF16)
            keep(mlcol, j * 4 + r2 * 2, peak, total)

        half_chunk(chunk, half, put_row, merges)
        ml_ref[half] = mlcol[...].T[0:16]

    mlcol[...] = jnp.zeros((128, 128), F32)

    def next_chunk(chunk):
        for copy in q_copies(chunk):
            copy.wait()
        if chunk < 3:
            for copy in q_copies(chunk + 1):
                copy.start()
        gather_tokens(chunk)

    next_chunk(0)
    send_half(0, 0, s_opp, m_opp, ())
    put(0, s_opp.at[0], r_opp0, up_u)
    put(1, m_opp.at[0], n_opp0, up_u)
    send_half(0, 1, s_opp, m_opp, ())
    put(2, s_opp.at[1], r_opp1, dn_u)
    put(3, m_opp.at[1], n_opp1, dn_u)

    next_chunk(1)
    send_half(1, 1, s_up, m_up, ())
    put(4, s_up.at[1], r_up.at[1], up_u)
    put(5, m_up.at[1], n_up.at[1], up_u)
    get(0, r_opp0)
    get(1, n_opp0)
    flip_in(0, n_opp0)
    send_half(1, 0, s_up, m_up, ((0, r_opp0),))
    put(6, s_up.at[0], r_up.at[0], up_u)
    put(7, m_up.at[0], n_up.at[0], up_u)

    next_chunk(2)
    send_half(2, 0, s_dn, m_dn, ())
    put(8, s_dn.at[0], r_dn.at[0], dn_u)
    put(9, m_dn.at[0], n_dn.at[0], dn_u)
    get(2, r_opp1)
    get(3, n_opp1)
    flip_in(0, n_opp1)
    send_half(2, 1, s_dn, m_dn, ((0, r_opp1),))
    put(10, s_dn.at[1], r_dn.at[1], dn_u)
    put(11, m_dn.at[1], n_dn.at[1], dn_u)

    next_chunk(3)
    for half in range(2):

        def put_row(j, r2, sums, peak, total):
            acc[j, half * 2 + r2] = sums
            keep(mlcol, j * 8 + half * 4 + r2 * 2, peak, total)

        half_chunk(3, half, put_row, ())

    for half in range(2):
        get(4 if half else 6, r_up.at[half])
        get(5 if half else 7, n_up.at[half])
        get(10 if half else 8, r_dn.at[half])
        get(11 if half else 9, n_dn.at[half])
        flip_in(half * 2, n_up.at[half])
        flip_in(half * 2 + 1, n_dn.at[half])

    def add_first(j, carry):
        for r in range(4):
            half, r2 = r // 2, r % 2
            at, here = j * 4 + r2 * 2, j * 8 + r * 2
            got = (acc[j, r], column(mlcol, here), column(mlcol, here + 1))
            for slot, ref in ((half * 2, r_up), (half * 2 + 1, r_dn)):
                got = joined(got, (ref[half, j, r2], column(mlin.at[slot], at), column(mlin.at[slot], at + 1)))
            acc[j, r] = got[0]
            keep(mlcol, here, got[1], got[2])
        return carry

    lax.fori_loop(0, 4, add_first, 0)

    def second_send(j, half, sums_ref, ml_ref, merge=None):
        if merge is not None:
            flip_in(0, merge[1])
        for r2 in range(2):
            r = half * 2 + r2
            at = j * 8 + r * 2
            got = (acc[j, r], column(mlcol, at), column(mlcol, at + 1))
            if merge is not None:
                got = joined(
                    got, (merge[0][r2], column(mlin.at[0], at % 8), column(mlin.at[0], at % 8 + 1))
                )
                keep(mlcol, at, got[1], got[2])
            sums_ref[half, r2] = got[0].astype(BF16)
        ml_ref[half] = mlcol[...].T[j * 8 : j * 8 + 8]

    second_send(0, 0, t_opp, e_opp)
    put(12, t_opp.at[0], w_opp0, up_v)
    put(13, e_opp.at[0], f_opp0, up_v)
    second_send(0, 1, t_opp, e_opp)
    put(14, t_opp.at[1], w_opp1, dn_v)
    put(15, e_opp.at[1], f_opp1, dn_v)
    second_send(1, 1, t_up, e_up)
    put(16, t_up.at[1], w_up.at[1], up_v)
    put(17, e_up.at[1], f_up.at[1], up_v)
    second_send(2, 0, t_dn, e_dn)
    put(20, t_dn.at[0], w_dn.at[0], dn_v)
    put(21, e_dn.at[0], f_dn.at[0], dn_v)
    get(12, w_opp0)
    get(13, f_opp0)
    second_send(1, 0, t_up, e_up, (w_opp0, f_opp0))
    put(18, t_up.at[0], w_up.at[0], up_v)
    put(19, e_up.at[0], f_up.at[0], up_v)
    get(14, w_opp1)
    get(15, f_opp1)
    second_send(2, 1, t_dn, e_dn, (w_opp1, f_opp1))
    put(22, t_dn.at[1], w_dn.at[1], dn_v)
    put(23, e_dn.at[1], f_dn.at[1], dn_v)

    for half in (1, 0):
        get(16 if half else 18, w_up.at[half])
        get(17 if half else 19, f_up.at[half])
        get(22 if half else 20, w_dn.at[half])
        get(23 if half else 21, f_dn.at[half])
        flip_in(half * 2, f_up.at[half])
        flip_in(half * 2 + 1, f_dn.at[half])
    for r in range(4):
        half, r2 = r // 2, r % 2
        at = 24 + r * 2
        got = (acc[3, r], column(mlcol, at), column(mlcol, at + 1))
        for slot, ref in ((half * 2, w_up), (half * 2 + 1, w_dn)):
            got = joined(got, (ref[half, r2], column(mlin.at[slot], r * 2), column(mlin.at[slot], r * 2 + 1)))
        out_ref[r] = (got[0] / got[2]).astype(BF16)
    for copy in sent:
        copy.wait_send()


def vmem():
    return pl.BlockSpec(memory_space=pltpu.VMEM)


def anywhere():
    return pl.BlockSpec(memory_space=pl.ANY)


def body(latent_cache, index_keys, query_latent, index_query, index_gates, selected):
    rows, heads, width = query_latent.shape
    tokens = latent_cache.shape[0]
    kt = latent_cache.T
    q_latent = query_latent[:, :, :LATENT].transpose(1, 0, 2).reshape(heads, rows * LATENT)
    q_rope = query_latent[:, :, LATENT:].transpose(1, 0, 2).reshape(heads, rows * (width - LATENT))
    qw = jnp.concatenate([q_latent, q_rope], axis=1)
    gates = jnp.pad(index_gates.T, ((0, 0), (0, 128 - rows)))
    iqg = jnp.concatenate([index_query.reshape(-1, 128), gates], axis=0)
    sel = selected.reshape(rows * 4, -1)
    dma = pltpu.SemaphoreType.DMA

    qall, kall, tall, index_scores = pl.pallas_call(
        gather_kernel,
        out_shape=(
            jax.ShapeDtypeStruct((16,) + qw.shape, BF16),
            jax.ShapeDtypeStruct((8, width, tokens), BF16),
            jax.ShapeDtypeStruct((16, 16, 128), BF16),
            jax.ShapeDtypeStruct((rows * 32, index_keys.shape[0]), F32),
        ),
        in_specs=[vmem()] * 5,
        out_specs=(anywhere(), anywhere(), anywhere(), vmem()),
        scratch_shapes=[
            pltpu.VMEM((16, 2) + iqg.shape, BF16),
            pltpu.VMEM((16, 16, 128), BF16),
            pltpu.VMEM((512, 128), F32),
            dma((20,)), dma((20,)), dma((20,)), dma((20,)), dma((21,)), dma((21,)),
            dma((9,)), dma((9,)), dma((16,)), dma((16,)), dma((4,)),
        ],
        compiler_params=pltpu.CompilerParams(
            collective_id=0, has_side_effects=True, vmem_limit_bytes=48 * 1024 * 1024
        ),
        name="gather",
    )(qw, kt, iqg, index_keys, sel)

    half = (4, 2, heads, LATENT)
    quarter = (2, heads, LATENT)
    attended = pl.pallas_call(
        attend_kernel,
        out_shape=jax.ShapeDtypeStruct((rows, heads, LATENT), BF16),
        in_specs=[anywhere(), anywhere(), vmem()],
        out_specs=vmem(),
        scratch_shapes=[
            pltpu.VMEM((32, 640, 256), BF16),
            pltpu.VMEM((16, 512, 640), BF16),
            pltpu.VMEM((2, 4) + qw.shape, BF16),
            pltpu.VMEM((256, 128), F32),
            pltpu.VMEM((128, 128), F32),
            pltpu.VMEM((4, 128, 128), F32),
        ]
        + [pltpu.VMEM((2,) + half, BF16)] * 3
        + [pltpu.VMEM(half, BF16)] * 2
        + [pltpu.VMEM((2,) + half, BF16)] * 2
        + [pltpu.VMEM((2, 16, 128), F32)] * 3
        + [pltpu.VMEM((16, 128), F32)] * 2
        + [pltpu.VMEM((2, 16, 128), F32)] * 2
        + [pltpu.VMEM((4, rows, heads, LATENT), F32)]
        + [pltpu.VMEM((2,) + quarter, BF16)] * 3
        + [pltpu.VMEM(quarter, BF16)] * 2
        + [pltpu.VMEM((2,) + quarter, BF16)] * 2
        + [pltpu.VMEM((2, 8, 128), F32)] * 3
        + [pltpu.VMEM((8, 128), F32)] * 2
        + [pltpu.VMEM((2, 8, 128), F32)] * 2
        + [dma((32,)), dma((2, 4)), dma((24,)), dma((24,))],
        compiler_params=pltpu.CompilerParams(
            collective_id=1, has_side_effects=True, vmem_limit_bytes=60 * 1024 * 1024
        ),
        name="attend",
    )(qall, kall, tall)
    return attended, index_scores


def solution(mesh):
    return jax.shard_map(
        body,
        mesh=mesh,
        in_specs=(
            P(("ctx", "row"), None),
            P("ctx", None),
            P(("row", "ctx"), None, None),
            P(("row", "ctx"), None, None),
            P(("row", "ctx"), None),
            P(("row", "ctx"), None),
        ),
        out_specs=(P(("row", "ctx"), None, None), P("row", "ctx")),
        check_vma=False,
    )
```

```python
import math

import jax
import jax.numpy as jnp
from jax import lax
from jax.experimental import pallas as pl
from jax.experimental.pallas import tpu as pltpu
from jax.sharding import PartitionSpec as P

MESH = pl.DeviceIdType.MESH
LATENT = 512
TO_LOG2 = 192 ** (-0.5) * math.log2(math.e)
NONE = -1e30
FLOOR = -1e29
F32 = jnp.float32
BF16 = jnp.bfloat16
NT = (((1,), (1,)), ((), ()))


def remote(src, dst, send, recv, device):
    return pltpu.make_async_remote_copy(
        src_ref=src, dst_ref=dst, send_sem=send, recv_sem=recv, device_id=device, device_id_type=MESH
    )


def place(core):
    chip = lax.axis_index("ctx") // 2
    x, y = chip // 4, chip % 4
    return x * (1 - core) + y * core, y * (1 - core) + x * core


def chip_of(a, b, core):
    a, b = a % 4, b % 4
    return (a * (1 - core) + b * core) * 4 + b * (1 - core) + a * core


class Ring:
    def __init__(self, own, buf, rows, send, recv, core, on_block=None):
        self.own, self.buf, self.send, self.recv, self.core = own, buf, send, recv, core
        self.halves = (pl.ds(0, rows), pl.ds(0, rows // 2), pl.ds(rows // 2, rows // 2))
        self.a, self.b = place(core)
        self.columns = (self.a, self.a + 3, self.a + 1, self.a + 2)
        self.sent = []
        self.on_block = on_block

    def view(self, a, b, part):
        return self.buf(chip_of(a, b, self.core), self.halves[part])

    def put(self, k, block, part, to, own=False):
        src = self.own if own else self.view(*block, part)
        device = {"ctx": chip_of(*to, self.core) * 2 + self.core}
        copy = remote(src, self.view(*block, part), self.send.at[k], self.recv.at[k], device)
        copy.start()
        self.sent.append(copy)

    def get(self, k, block, part, event):
        ref = self.view(*block, part)
        remote(ref, ref, self.send.at[k], self.recv.at[k], {"ctx": lax.axis_index("ctx")}).wait_recv()
        if self.on_block is not None:
            self.on_block(event, block, part)

    def start(self):
        a, b = self.a, self.b
        self.put(4, (a, b), 0, (a, b + 1), own=True)
        self.put(5, (a, b), 0, (a, b + 3), own=True)
        self.put(0, (a, b), 0, (a + 1, b), own=True)
        self.put(1, (a, b), 0, (a + 3, b), own=True)

    def second(self, j):
        block = (self.columns[j], self.b)
        self.put(4 + 4 * j, block, 0, (self.a, self.b + 1))
        self.put(5 + 4 * j, block, 0, (self.a, self.b + 3))

    def near(self):
        a, b = self.a, self.b
        self.get(0, (a + 3, b), 0, 1)
        self.put(2, (a + 3, b), 1, (a + 1, b))
        self.second(1)
        self.get(1, (a + 1, b), 0, 2)
        self.put(3, (a + 1, b), 2, (a + 3, b))
        self.second(2)

    def far(self):
        a, b = self.a, self.b
        self.get(2, (a + 2, b), 1, 3)
        self.get(3, (a + 2, b), 2, 4)
        self.second(3)

    def relay(self, j):
        column, b = self.columns[j], self.b
        self.get(4 + 4 * j, (column, b + 3), 0, 5 + 4 * j)
        self.put(6 + 4 * j, (column, b + 3), 1, (self.a, b + 1))
        self.get(5 + 4 * j, (column, b + 1), 0, 6 + 4 * j)
        self.put(7 + 4 * j, (column, b + 1), 2, (self.a, b + 3))

    def last(self, j):
        column, b = self.columns[j], self.b
        self.get(6 + 4 * j, (column, b + 2), 1, 7 + 4 * j)
        self.get(7 + 4 * j, (column, b + 2), 2, 8 + 4 * j)

    def finish(self):
        for copy in self.sent:
            copy.wait_send()


def gather_kernel(
    q_ref, k_ref, iq_ref, keys_hbm, sel_ref,
    qall, kall, tall, isc_ref,
    iqall, tsend, gate_ref, keys_ref, logit_ref,
    q_send, q_recv, i_send, i_recv, p_send, p_recv, k_send, k_recv, t_send, t_recv, local,
):
    ctx, z = lax.axis_index("ctx"), lax.axis_index("row")
    core, chip = ctx % 2, ctx // 2
    other = 1 - core
    partner = {"ctx": chip * 2 + other}
    x, y = chip // 4, chip % 4

    keys_copy = pltpu.make_async_copy(keys_hbm, keys_ref, local.at[4])
    keys_copy.start()
    barrier = pltpu.get_barrier_semaphore()
    for step in range(1, 16):
        pl.semaphore_signal(
            barrier, inc=1, device_id={"ctx": ((chip + step) % 16) * 2 + core}, device_id_type=MESH
        )
    pl.semaphore_signal(barrier, inc=1, device_id=partner, device_id_type=MESH)
    for step in (1, 3):
        pl.semaphore_signal(barrier, inc=1, device_id={"row": (z + step) % 4}, device_id_type=MESH)
    pl.semaphore_wait(barrier, 18)

    to_partner = []

    def hand_on(event, block, part):
        ref = index_ring.view(*block, part)
        copy = remote(ref, ref, p_send.at[event], p_recv.at[event], partner)
        copy.start()
        to_partner.append(copy)

    index_ring = Ring(
        iq_ref, lambda p, rows: iqall.at[p, core, rows], iq_ref.shape[0], i_send, i_recv, core, hand_on
    )
    index_ring.start()
    copy = remote(iq_ref, iqall.at[chip, core], p_send.at[0], p_recv.at[0], partner)
    copy.start()
    to_partner.append(copy)

    k_rows = k_ref.shape[0]
    parts = (pl.ds(0, k_rows), pl.ds(0, k_rows // 2), pl.ds(k_rows // 2, k_rows // 2))
    k_sent = []

    def k_view(depth, part, c=core):
        return kall.at[c * 4 + depth % 4, parts[part]]

    def k_put(k, src, dst, device):
        copy = remote(src, dst, k_send.at[k], k_recv.at[k], device)
        copy.start()
        k_sent.append(copy)

    def k_get(k, depth, part, c=core):
        ref = k_view(depth, part, c)
        remote(ref, ref, k_send.at[k], k_recv.at[k], {"row": z}).wait_recv()

    up, down = {"row": (z + 1) % 4}, {"row": (z + 3) % 4}
    query_ring = Ring(q_ref, lambda p, rows: qall.at[p, rows], q_ref.shape[0], q_send, q_recv, core)
    query_ring.start()
    k_put(0, k_ref, k_view(z, 0), up)
    k_put(1, k_ref, k_view(z, 0), down)
    k_put(4, k_ref, k_view(z, 0), partner)

    own = [
        pltpu.make_async_copy(iq_ref, iqall.at[chip, core], local.at[3]),
        pltpu.make_async_copy(q_ref, qall.at[chip], local.at[0]),
        pltpu.make_async_copy(k_ref, k_view(z, 0), local.at[1]),
    ]
    for copy in own:
        copy.start()

    pieces = sel_ref.shape[1] // 512

    def add_picks(i, total):
        at = pl.ds(pl.multiple_of((i % pieces) * 512, 512), 512)
        token = sel_ref[pl.ds(i // pieces, 1), at]
        to = (token >> 13) * 16 + ((token >> 4) & 15)
        window = (i // pieces) * 32 + ((token >> 8) & 31)
        value = ((token & 255) + 1).astype(F32)
        left = lax.broadcasted_iota(jnp.int32, (256, 512), 0) == to
        right = lax.broadcasted_iota(jnp.int32, (128, 512), 0) == window
        return total + lax.dot_general(
            jnp.where(left, 1.0, 0.0).astype(BF16),
            jnp.where(right, value, 0.0).astype(BF16),
            NT,
            preferred_element_type=F32,
        )

    table = lax.fori_loop(0, sel_ref.shape[0] * pieces, add_picks, jnp.zeros((256, 128), F32))
    tsend[...] = table.astype(BF16).reshape(16, 16, 128)

    table_copies = []

    def send_tables():
        for step in range(1, 16):
            to = (chip + step) % 16
            copy = remote(
                tsend.at[to], tall.at[chip], t_send.at[step], t_recv.at[step], {"ctx": to * 2 + core}
            )
            copy.start()
            table_copies.append(copy)
        own.append(pltpu.make_async_copy(tsend.at[chip], tall.at[chip], local.at[2]))
        own[-1].start()

    oa, ob = place(other)
    columns = (0, 3, 1, 2)

    def wait_partner(da, db):
        if db:
            j = columns.index(da)
            events = {3: ((5 + 4 * j, 0),), 1: ((6 + 4 * j, 0),), 2: ((7 + 4 * j, 1), (8 + 4 * j, 2))}[db]
        else:
            events = {0: ((0, 0),), 3: ((1, 0),), 1: ((2, 0),), 2: ((3, 1), (4, 2))}[da]
        for event, part in events:
            ref = iqall.at[chip_of(oa + da, ob + db, other), other, index_ring.halves[part]]
            remote(ref, ref, p_send.at[event], p_recv.at[event], partner).wait_recv()

    tile = 512
    tiles = keys_ref.shape[0] // tile

    def index_chip(p):
        for c in range(2):
            gates = iqall[p, c, 256:320, :].astype(F32)
            for r in range(4):
                gate_ref[pl.ds((c * 4 + r) * 64, 64), :] = jnp.broadcast_to(gates[:, r : r + 1], (64, 128))

        def token_tile(t):
            return pl.ds(pl.multiple_of(t * tile, tile), tile)

        def logits(t, slot):
            logit_ref[slot] = lax.dot_general(
                iqall[p, :, 0:256, :].reshape(512, 128), keys_ref[token_tile(t), :], NT, preferred_element_type=F32
            )

        def gated_sum(t, slot):
            columns = []
            for lanes in range(0, tile, 128):
                rows = []
                for i in range(8):
                    total = None
                    for h in range(0, 64, 8):
                        part = logit_ref[slot, i * 64 + h : i * 64 + h + 8, lanes : lanes + 128]
                        part = jnp.maximum(part, 0.0) * gate_ref[i * 64 + h : i * 64 + h + 8, :]
                        total = part if total is None else total + part
                    rows.append(jnp.sum(total, axis=0, keepdims=True))
                columns.append(jnp.concatenate(rows, axis=0))
            isc_ref[pl.ds(pl.multiple_of(p * 8, 8), 8), token_tile(t)] = jnp.concatenate(columns, axis=1)

        logits(0, 0)

        def two_tiles(i, carry):
            logits(i * 2 + 1, 1)
            gated_sum(i * 2, 0)
            logits(jnp.minimum(i * 2 + 2, tiles - 1), 0)
            gated_sum(i * 2 + 1, 1)
            return carry

        lax.fori_loop(0, tiles // 2, two_tiles, 0)

    def index_chips(low, high, dx, dy):
        def one(k, carry):
            index_chip((x + dx(k)) % 4 * 4 + (y + dy(k)) % 4)
            return carry

        lax.fori_loop(low, high, one, 0)

    beside = (lambda k: (1 - k // 2) * (1 + 2 * (k % 2)), lambda k: (k // 2) * (1 + 2 * (k % 2)))
    corner = (lambda k: 1 + 2 * (k % 2), lambda k: 1 + 2 * (k // 2))
    rest = (
        lambda k: 2 * (k == 0) + 2 * (k == 2) + 2 * (k == 3) + (k == 4) + 3 * (k == 5) + 2 * (k == 6),
        lambda k: 2 * (k == 1) + (k == 2) + 3 * (k == 3) + 2 * (k == 4) + 2 * (k == 5) + 2 * (k == 6),
    )

    index_ring.near()
    send_tables()
    index_ring.relay(0)
    index_ring.far()
    own[0].wait()
    keys_copy.wait()
    wait_partner(0, 0)
    index_chips(0, 1, lambda k: k, lambda k: k)
    index_ring.relay(1)
    index_ring.relay(2)
    index_ring.last(0)
    index_ring.relay(3)
    for j in (1, 2, 3):
        index_ring.last(j)
    query_ring.near()
    query_ring.relay(0)
    for da, db in ((3, 0), (1, 0), (0, 3), (0, 1)):
        wait_partner(da, db)
    index_chips(0, 4, *beside)
    query_ring.far()
    k_get(0, z + 3, 0)
    k_put(2, k_view(z + 3, 1), k_view(z + 3, 1), up)
    k_put(5, k_view(z + 3, 0), k_view(z + 3, 0), partner)
    k_get(1, z + 1, 0)
    k_put(3, k_view(z + 1, 2), k_view(z + 1, 2), down)
    k_put(6, k_view(z + 1, 0), k_view(z + 1, 0), partner)
    for da, db in ((3, 3), (3, 1), (1, 3), (1, 1)):
        wait_partner(da, db)
    index_chips(0, 2, *corner)
    query_ring.relay(1)
    query_ring.relay(2)
    index_chips(2, 4, *corner)
    for da, db in ((2, 0), (0, 2), (3, 2), (1, 2), (2, 3), (2, 1), (2, 2)):
        wait_partner(da, db)
    index_chips(0, 3, *rest)
    query_ring.relay(3)
    k_get(2, z + 2, 1)
    k_put(7, k_view(z + 2, 1), k_view(z + 2, 1), partner)
    k_get(3, z + 2, 2)
    k_put(8, k_view(z + 2, 2), k_view(z + 2, 2), partner)
    index_chips(3, 7, *rest)

    for j in range(4):
        query_ring.last(j)
    k_get(4, z, 0, other)
    k_get(5, z + 3, 0, other)
    k_get(6, z + 1, 0, other)
    k_get(7, z + 2, 1, other)
    k_get(8, z + 2, 2, other)
    for step in range(1, 16):
        frm = (chip + 16 - step) % 16
        remote(
            tall.at[frm], tall.at[frm], t_send.at[step], t_recv.at[step], partner
        ).wait_recv()
    for copy in own[1:]:
        copy.wait()
    query_ring.finish()
    index_ring.finish()
    for copy in to_partner + table_copies + k_sent:
        copy.wait_send()


def attend_kernel(
    qall, kall, tall, out_ref,
    kext, ksel, qbuf, rope, raw, picks, mlcol, mlin,
    s_opp, s_up, s_dn, r_opp0, r_opp1, r_up, r_dn,
    m_opp, m_up, m_dn, n_opp0, n_opp1, n_up, n_dn,
    acc, t_opp, t_up, t_dn, w_opp0, w_opp1, w_up, w_dn,
    e_opp, e_up, e_dn, f_opp0, f_opp1, f_up, f_dn,
    k_sem, q_sem, send, recv,
):
    ctx = lax.axis_index("ctx")
    core = ctx % 2
    u, v = place(core)
    up_u = {"ctx": chip_of(u + 1, v, core) * 2 + core}
    dn_u = {"ctx": chip_of(u + 3, v, core) * 2 + core}
    up_v = {"ctx": chip_of(u, v + 1, core) * 2 + core}
    dn_v = {"ctx": chip_of(u, v + 3, core) * 2 + core}
    order = (2, 1, 3, 0)

    barrier = pltpu.get_barrier_semaphore()
    for device in (up_u, dn_u, up_v, dn_v):
        pl.semaphore_signal(barrier, inc=1, device_id=device, device_id_type=MESH)

    def k_copy(w):
        at = pl.ds(pl.multiple_of((w % 4) * 256, 256), 256)
        return pltpu.make_async_copy(kall.at[w // 4, :, at], kext.at[w, pl.ds(0, 576), :], k_sem.at[w])

    def q_copies(chunk):
        return [
            pltpu.make_async_copy(
                qall.at[chip_of(u + order[chunk], v + order[j], core), :, pl.ds(r * 512, width)],
                qbuf.at[chunk % 2, j * 4 + r, pl.ds(0, 128), pl.ds(0, 512)]
                if r < 4
                else rope.at[chunk % 2, j],
                q_sem.at[chunk % 2, j * 5 + r],
            )
            for j in range(4)
            for r, width in ((0, 512), (1, 512), (2, 512), (3, 512), (4, 256))
        ]

    def start_k(w, carry):
        k_copy(w).start()
        return carry

    lax.fori_loop(0, 32, start_k, 0)
    for copy in q_copies(0):
        copy.start()

    ones = jnp.where(lax.broadcasted_iota(jnp.int32, (64, 256), 0) == 0, 1.0, 0.0).astype(BF16)

    def set_ones(w, carry):
        kext[w, pl.ds(576, 64), :] = ones
        return carry

    lax.fori_loop(0, 32, set_ones, 0)
    probe = jnp.where(lax.broadcasted_iota(jnp.int32, (16, 640), 1) == 576, 1.0, 0.0).astype(BF16)

    def set_probe(row, carry):
        for slot in range(2):
            qbuf[slot, row, pl.ds(128, 16), :] = probe
        return carry

    lax.fori_loop(0, 16, set_probe, 0)
    pl.semaphore_wait(barrier, 4)

    sent = []

    def put(k, src, dst, device):
        copy = remote(src, dst, send.at[k], recv.at[k], device)
        copy.start()
        sent.append(copy)

    def get(k, ref):
        remote(ref, ref, send.at[k], recv.at[k], up_u).wait_recv()

    lane = lax.broadcasted_iota(jnp.int32, (128, 128), 1)

    def column(ref, at):
        return jnp.sum(jnp.where(lane == at, ref[...], 0.0), axis=1, keepdims=True)

    def keep(ref, at, peak, total):
        ref[...] = jnp.where(lane == at, peak, jnp.where(lane == at + 1, total, ref[...]))

    def flip_in(slot, ref):
        rows = ref.shape[0]
        full = jnp.concatenate([ref[...], jnp.zeros((128 - rows, 128), F32)], axis=0)
        mlin[slot] = full.T

    def joined(one, two):
        sums1, peak1, total1 = one
        sums2, peak2, total2 = two
        peak = jnp.maximum(peak1, peak2)
        f1, f2 = jnp.exp2((peak1 - peak) * TO_LOG2), jnp.exp2((peak2 - peak) * TO_LOG2)
        return sums1 * f1 + sums2.astype(F32) * f2, peak, total1 * f1 + total2 * f2

    def gather_tokens(chunk):
        for j in range(4):
            t = tall[chip_of(u + order[chunk], v + order[j], core)].astype(F32)
            for r in range(4):
                moved = t if r == 0 else pltpu.roll(t, 128 - r * 32, axis=1)
                picks[pl.ds((j * 4 + r) * 16, 16), :] = moved
        wide = lax.broadcasted_iota(jnp.int32, (256, 128), 1)
        token = (lax.broadcasted_iota(jnp.int32, (256, 256), 1) + 1).astype(F32)

        def some_windows(i, carry):
            for step in range(4):
                w = i * 4 + step
                if chunk == 0:
                    k_copy(w).wait()
            for step in range(4):
                w = i * 4 + step
                want = jnp.sum(jnp.where(wide == w, picks[...], 0.0), axis=1, keepdims=True)
                onehot = jnp.where(token == want, 1.0, 0.0).astype(BF16)
                rows = lax.dot_general(onehot, kext[w], NT, preferred_element_type=F32)
                at = pl.ds(pl.multiple_of(w * 16, 16), 16)
                ksel[:, at, :] = rows.astype(BF16).reshape(16, 16, 640)
            return carry

        lax.fori_loop(0, 8, some_windows, 0)

    def set_rope(slot):
        def one_block(j, carry):
            for r in range(4):
                part = rope[slot, j, :, r * 64 : (r + 1) * 64]
                qbuf[slot, j * 4 + r, pl.ds(0, 128), pl.ds(512, 128)] = jnp.concatenate(
                    [part, jnp.zeros((128, 64), BF16)], axis=1
                )
            return carry

        lax.fori_loop(0, 4, one_block, 0)

    def score_row(slot, row, to):
        raw[to] = lax.dot_general(qbuf[slot, row], ksel[row], NT, preferred_element_type=F32)

    def attend_row(row, frm):
        scores = jnp.where(raw[frm, 128:129, :] > 0.5, raw[frm, 0:128, :], NONE)
        peak = jnp.maximum(jnp.max(scores, axis=1, keepdims=True), FLOOR)
        weights = jnp.exp2((scores - peak) * TO_LOG2)
        total = jnp.sum(weights, axis=1, keepdims=True)
        sums = jnp.dot(weights.astype(BF16), ksel[row, :, 0:512], preferred_element_type=F32)
        return sums, peak, total

    def half_chunk(chunk, half, put_row, merges):
        slot = chunk % 2
        score_row(slot, half * 2, 0)

        def one_block(j, carry):
            for r2 in range(2):
                row = j * 4 + half * 2 + r2
                score_row(slot, (row + 1 if r2 == 0 else jnp.minimum(row + 3, 12 + half * 2)), 1 - r2)
                got = attend_row(row, r2)
                for at_slot, ref in merges:
                    at = j * 4 + r2 * 2
                    got = joined(
                        got, (ref[j, r2], column(mlin.at[at_slot], at), column(mlin.at[at_slot], at + 1))
                    )
                put_row(j, r2, *got)
            return carry

        lax.fori_loop(0, 4, one_block, 0)

    def send_half(chunk, half, sums_ref, ml_ref, merges):
        def put_row(j, r2, sums, peak, total):
            sums_ref[half, j, r2] = sums.astype(BF16)
            keep(mlcol, j * 4 + r2 * 2, peak, total)

        half_chunk(chunk, half, put_row, merges)
        ml_ref[half] = mlcol[...].T[0:16]

    mlcol[...] = jnp.zeros((128, 128), F32)

    def next_chunk(chunk):
        for copy in q_copies(chunk):
            copy.wait()
        if chunk < 3:
            for copy in q_copies(chunk + 1):
                copy.start()
        set_rope(chunk % 2)
        gather_tokens(chunk)

    next_chunk(0)
    send_half(0, 0, s_opp, m_opp, ())
    put(0, s_opp.at[0], r_opp0, up_u)
    put(1, m_opp.at[0], n_opp0, up_u)
    send_half(0, 1, s_opp, m_opp, ())
    put(2, s_opp.at[1], r_opp1, dn_u)
    put(3, m_opp.at[1], n_opp1, dn_u)

    next_chunk(1)
    send_half(1, 1, s_up, m_up, ())
    put(4, s_up.at[1], r_up.at[1], up_u)
    put(5, m_up.at[1], n_up.at[1], up_u)
    get(0, r_opp0)
    get(1, n_opp0)
    flip_in(0, n_opp0)
    send_half(1, 0, s_up, m_up, ((0, r_opp0),))
    put(6, s_up.at[0], r_up.at[0], up_u)
    put(7, m_up.at[0], n_up.at[0], up_u)

    next_chunk(2)
    send_half(2, 0, s_dn, m_dn, ())
    put(8, s_dn.at[0], r_dn.at[0], dn_u)
    put(9, m_dn.at[0], n_dn.at[0], dn_u)
    get(2, r_opp1)
    get(3, n_opp1)
    flip_in(0, n_opp1)
    send_half(2, 1, s_dn, m_dn, ((0, r_opp1),))
    put(10, s_dn.at[1], r_dn.at[1], dn_u)
    put(11, m_dn.at[1], n_dn.at[1], dn_u)

    next_chunk(3)
    for half in range(2):

        def put_row(j, r2, sums, peak, total):
            acc[j, half * 2 + r2] = sums
            keep(mlcol, j * 8 + half * 4 + r2 * 2, peak, total)

        half_chunk(3, half, put_row, ())

    for half in range(2):
        get(4 if half else 6, r_up.at[half])
        get(5 if half else 7, n_up.at[half])
        get(10 if half else 8, r_dn.at[half])
        get(11 if half else 9, n_dn.at[half])
        flip_in(half * 2, n_up.at[half])
        flip_in(half * 2 + 1, n_dn.at[half])

    def add_first(j, carry):
        for r in range(4):
            half, r2 = r // 2, r % 2
            at, here = j * 4 + r2 * 2, j * 8 + r * 2
            got = (acc[j, r], column(mlcol, here), column(mlcol, here + 1))
            for slot, ref in ((half * 2, r_up), (half * 2 + 1, r_dn)):
                got = joined(got, (ref[half, j, r2], column(mlin.at[slot], at), column(mlin.at[slot], at + 1)))
            acc[j, r] = got[0]
            keep(mlcol, here, got[1], got[2])
        return carry

    lax.fori_loop(0, 4, add_first, 0)

    def second_send(j, half, sums_ref, ml_ref, merge=None):
        if merge is not None:
            flip_in(0, merge[1])
        for r2 in range(2):
            r = half * 2 + r2
            at = j * 8 + r * 2
            got = (acc[j, r], column(mlcol, at), column(mlcol, at + 1))
            if merge is not None:
                got = joined(
                    got, (merge[0][r2], column(mlin.at[0], at % 8), column(mlin.at[0], at % 8 + 1))
                )
                keep(mlcol, at, got[1], got[2])
            sums_ref[half, r2] = got[0].astype(BF16)
        ml_ref[half] = mlcol[...].T[j * 8 : j * 8 + 8]

    second_send(0, 0, t_opp, e_opp)
    put(12, t_opp.at[0], w_opp0, up_v)
    put(13, e_opp.at[0], f_opp0, up_v)
    second_send(0, 1, t_opp, e_opp)
    put(14, t_opp.at[1], w_opp1, dn_v)
    put(15, e_opp.at[1], f_opp1, dn_v)
    second_send(1, 1, t_up, e_up)
    put(16, t_up.at[1], w_up.at[1], up_v)
    put(17, e_up.at[1], f_up.at[1], up_v)
    second_send(2, 0, t_dn, e_dn)
    put(20, t_dn.at[0], w_dn.at[0], dn_v)
    put(21, e_dn.at[0], f_dn.at[0], dn_v)
    get(12, w_opp0)
    get(13, f_opp0)
    second_send(1, 0, t_up, e_up, (w_opp0, f_opp0))
    put(18, t_up.at[0], w_up.at[0], up_v)
    put(19, e_up.at[0], f_up.at[0], up_v)
    get(14, w_opp1)
    get(15, f_opp1)
    second_send(2, 1, t_dn, e_dn, (w_opp1, f_opp1))
    put(22, t_dn.at[1], w_dn.at[1], dn_v)
    put(23, e_dn.at[1], f_dn.at[1], dn_v)

    for half in (1, 0):
        get(16 if half else 18, w_up.at[half])
        get(17 if half else 19, f_up.at[half])
        get(22 if half else 20, w_dn.at[half])
        get(23 if half else 21, f_dn.at[half])
        flip_in(half * 2, f_up.at[half])
        flip_in(half * 2 + 1, f_dn.at[half])
    for r in range(4):
        half, r2 = r // 2, r % 2
        at = 24 + r * 2
        got = (acc[3, r], column(mlcol, at), column(mlcol, at + 1))
        for slot, ref in ((half * 2, w_up), (half * 2 + 1, w_dn)):
            got = joined(got, (ref[half, r2], column(mlin.at[slot], r * 2), column(mlin.at[slot], r * 2 + 1)))
        out_ref[r] = (got[0] / got[2]).astype(BF16)
    for copy in sent:
        copy.wait_send()


def vmem():
    return pl.BlockSpec(memory_space=pltpu.VMEM)


def anywhere():
    return pl.BlockSpec(memory_space=pl.ANY)


def body(latent_cache, index_keys, query_latent, index_query, index_gates, selected):
    rows, heads, width = query_latent.shape
    tokens = latent_cache.shape[0]
    kt = latent_cache.T
    q_latent = query_latent[:, :, :LATENT].transpose(1, 0, 2).reshape(heads, rows * LATENT)
    q_rope = query_latent[:, :, LATENT:].transpose(1, 0, 2).reshape(heads, rows * (width - LATENT))
    qw = jnp.concatenate([q_latent, q_rope], axis=1)
    gates = jnp.pad(index_gates.T, ((0, 0), (0, 128 - rows)))
    iqg = jnp.concatenate([index_query.reshape(-1, 128), gates], axis=0)
    dma = pltpu.SemaphoreType.DMA

    qall, kall, tall, index_scores = pl.pallas_call(
        gather_kernel,
        out_shape=(
            jax.ShapeDtypeStruct((16,) + qw.shape, BF16),
            jax.ShapeDtypeStruct((8, width, tokens), BF16),
            jax.ShapeDtypeStruct((16, 16, 128), BF16),
            jax.ShapeDtypeStruct((rows * 32, index_keys.shape[0]), F32),
        ),
        in_specs=[vmem(), vmem(), vmem(), anywhere(), vmem()],
        out_specs=(anywhere(), anywhere(), anywhere(), vmem()),
        scratch_shapes=[
            pltpu.VMEM((16, 2) + iqg.shape, BF16),
            pltpu.VMEM((16, 16, 128), BF16),
            pltpu.VMEM((512, 128), F32),
            pltpu.VMEM(index_keys.shape, BF16),
            pltpu.VMEM((2, 512, 512), F32),
            dma((20,)), dma((20,)), dma((20,)), dma((20,)), dma((21,)), dma((21,)),
            dma((9,)), dma((9,)), dma((16,)), dma((16,)), dma((5,)),
        ],
        compiler_params=pltpu.CompilerParams(
            collective_id=0, has_side_effects=True, vmem_limit_bytes=48 * 1024 * 1024
        ),
        name="gather",
    )(qw, kt, iqg, index_keys, selected)

    half = (4, 2, heads, LATENT)
    quarter = (2, heads, LATENT)
    attended = pl.pallas_call(
        attend_kernel,
        out_shape=jax.ShapeDtypeStruct((rows, heads, LATENT), BF16),
        in_specs=[anywhere(), anywhere(), vmem()],
        out_specs=vmem(),
        scratch_shapes=[
            pltpu.VMEM((32, 640, 256), BF16),
            pltpu.VMEM((16, 512, 640), BF16),
            pltpu.VMEM((2, 16, 144, 640), BF16),
            pltpu.VMEM((2, 4, heads, 256), BF16),
            pltpu.VMEM((2, 144, 512), F32),
            pltpu.VMEM((256, 128), F32),
            pltpu.VMEM((128, 128), F32),
            pltpu.VMEM((4, 128, 128), F32),
        ]
        + [pltpu.VMEM((2,) + half, BF16)] * 3
        + [pltpu.VMEM(half, BF16)] * 2
        + [pltpu.VMEM((2,) + half, BF16)] * 2
        + [pltpu.VMEM((2, 16, 128), F32)] * 3
        + [pltpu.VMEM((16, 128), F32)] * 2
        + [pltpu.VMEM((2, 16, 128), F32)] * 2
        + [pltpu.VMEM((4, rows, heads, LATENT), F32)]
        + [pltpu.VMEM((2,) + quarter, BF16)] * 3
        + [pltpu.VMEM(quarter, BF16)] * 2
        + [pltpu.VMEM((2,) + quarter, BF16)] * 2
        + [pltpu.VMEM((2, 8, 128), F32)] * 3
        + [pltpu.VMEM((8, 128), F32)] * 2
        + [pltpu.VMEM((2, 8, 128), F32)] * 2
        + [dma((32,)), dma((2, 20)), dma((24,)), dma((24,))],
        compiler_params=pltpu.CompilerParams(
            collective_id=1, has_side_effects=True, vmem_limit_bytes=60 * 1024 * 1024
        ),
        name="attend",
    )(qall, kall, tall)
    return attended, index_scores


def solution(mesh):
    return jax.shard_map(
        body,
        mesh=mesh,
        in_specs=(
            P(("ctx", "row"), None),
            P("ctx", None),
            P(("row", "ctx"), None, None),
            P(("row", "ctx"), None, None),
            P(("row", "ctx"), None),
            P(("row", "ctx"), None),
        ),
        out_specs=(P(("row", "ctx"), None, None), P("row", "ctx")),
        check_vma=False,
    )
```

```python
import math

import jax
import jax.numpy as jnp
from jax import lax
from jax.experimental import pallas as pl
from jax.experimental.pallas import tpu as pltpu
from jax.sharding import PartitionSpec as P

MESH = pl.DeviceIdType.MESH
LATENT = 512
TO_LOG2 = 192 ** (-0.5) * math.log2(math.e)
NONE = -1e30
FLOOR = -1e29
F32 = jnp.float32
BF16 = jnp.bfloat16
NT = (((1,), (1,)), ((), ()))


def remote(src, dst, send, recv, device):
    return pltpu.make_async_remote_copy(
        src_ref=src, dst_ref=dst, send_sem=send, recv_sem=recv, device_id=device, device_id_type=MESH
    )


def place(core):
    chip = lax.axis_index("ctx") // 2
    x, y = chip // 4, chip % 4
    return x * (1 - core) + y * core, y * (1 - core) + x * core


def chip_of(a, b, core):
    a, b = a % 4, b % 4
    return (a * (1 - core) + b * core) * 4 + b * (1 - core) + a * core


class Ring:
    def __init__(self, own, buf, rows, send, recv, core, on_block=None):
        self.own, self.buf, self.send, self.recv, self.core = own, buf, send, recv, core
        self.halves = (pl.ds(0, rows), pl.ds(0, rows // 2), pl.ds(rows // 2, rows // 2))
        self.a, self.b = place(core)
        self.columns = (self.a, self.a + 3, self.a + 1, self.a + 2)
        self.sent = []
        self.on_block = on_block

    def view(self, a, b, part):
        return self.buf(chip_of(a, b, self.core), self.halves[part])

    def put(self, k, block, part, to, own=False):
        src = self.own if own else self.view(*block, part)
        device = {"ctx": chip_of(*to, self.core) * 2 + self.core}
        copy = remote(src, self.view(*block, part), self.send.at[k], self.recv.at[k], device)
        copy.start()
        self.sent.append(copy)

    def get(self, k, block, part, event):
        ref = self.view(*block, part)
        remote(ref, ref, self.send.at[k], self.recv.at[k], {"ctx": lax.axis_index("ctx")}).wait_recv()
        if self.on_block is not None:
            self.on_block(event, block, part)

    def start(self):
        a, b = self.a, self.b
        self.put(4, (a, b), 0, (a, b + 1), own=True)
        self.put(5, (a, b), 0, (a, b + 3), own=True)
        self.put(0, (a, b), 0, (a + 1, b), own=True)
        self.put(1, (a, b), 0, (a + 3, b), own=True)

    def second(self, j):
        block = (self.columns[j], self.b)
        self.put(4 + 4 * j, block, 0, (self.a, self.b + 1))
        self.put(5 + 4 * j, block, 0, (self.a, self.b + 3))

    def near(self):
        a, b = self.a, self.b
        self.get(0, (a + 3, b), 0, 1)
        self.put(2, (a + 3, b), 1, (a + 1, b))
        self.second(1)
        self.get(1, (a + 1, b), 0, 2)
        self.put(3, (a + 1, b), 2, (a + 3, b))
        self.second(2)

    def far(self):
        a, b = self.a, self.b
        self.get(2, (a + 2, b), 1, 3)
        self.get(3, (a + 2, b), 2, 4)
        self.second(3)

    def relay(self, j):
        column, b = self.columns[j], self.b
        self.get(4 + 4 * j, (column, b + 3), 0, 5 + 4 * j)
        self.put(6 + 4 * j, (column, b + 3), 1, (self.a, b + 1))
        self.get(5 + 4 * j, (column, b + 1), 0, 6 + 4 * j)
        self.put(7 + 4 * j, (column, b + 1), 2, (self.a, b + 3))

    def last(self, j):
        column, b = self.columns[j], self.b
        self.get(6 + 4 * j, (column, b + 2), 1, 7 + 4 * j)
        self.get(7 + 4 * j, (column, b + 2), 2, 8 + 4 * j)

    def finish(self):
        for copy in self.sent:
            copy.wait_send()


def gather_kernel(
    q_ref, k_ref, iq_ref, keys_hbm, sel_ref,
    qall, kall, tall, isc_ref,
    iqall, tsend, gate_ref, keys_ref, logit_ref,
    q_send, q_recv, i_send, i_recv, p_send, p_recv, k_send, k_recv, t_send, t_recv, local,
):
    ctx, z = lax.axis_index("ctx"), lax.axis_index("row")
    core, chip = ctx % 2, ctx // 2
    other = 1 - core
    partner = {"ctx": chip * 2 + other}
    x, y = chip // 4, chip % 4

    keys_copy = pltpu.make_async_copy(keys_hbm, keys_ref, local.at[4])
    keys_copy.start()
    barrier = pltpu.get_barrier_semaphore()
    for step in range(1, 16):
        pl.semaphore_signal(
            barrier, inc=1, device_id={"ctx": ((chip + step) % 16) * 2 + core}, device_id_type=MESH
        )
    pl.semaphore_signal(barrier, inc=1, device_id=partner, device_id_type=MESH)
    for step in (1, 3):
        pl.semaphore_signal(barrier, inc=1, device_id={"row": (z + step) % 4}, device_id_type=MESH)
    pl.semaphore_wait(barrier, 18)

    to_partner = []

    def hand_on(event, block, part):
        ref = index_ring.view(*block, part)
        copy = remote(ref, ref, p_send.at[event], p_recv.at[event], partner)
        copy.start()
        to_partner.append(copy)

    index_ring = Ring(
        iq_ref, lambda p, rows: iqall.at[p, core, rows], iq_ref.shape[0], i_send, i_recv, core, hand_on
    )
    index_ring.start()
    copy = remote(iq_ref, iqall.at[chip, core], p_send.at[0], p_recv.at[0], partner)
    copy.start()
    to_partner.append(copy)

    k_rows = k_ref.shape[0]
    parts = (pl.ds(0, k_rows), pl.ds(0, k_rows // 2), pl.ds(k_rows // 2, k_rows // 2))
    k_sent = []

    def k_view(depth, part, c=core):
        return kall.at[c * 4 + depth % 4, parts[part]]

    def k_put(k, src, dst, device):
        copy = remote(src, dst, k_send.at[k], k_recv.at[k], device)
        copy.start()
        k_sent.append(copy)

    def k_get(k, depth, part, c=core):
        ref = k_view(depth, part, c)
        remote(ref, ref, k_send.at[k], k_recv.at[k], {"row": z}).wait_recv()

    up, down = {"row": (z + 1) % 4}, {"row": (z + 3) % 4}
    query_ring = Ring(q_ref, lambda p, rows: qall.at[p, rows], q_ref.shape[0], q_send, q_recv, core)
    query_ring.start()
    k_put(0, k_ref, k_view(z, 0), up)
    k_put(1, k_ref, k_view(z, 0), down)
    k_put(4, k_ref, k_view(z, 0), partner)

    own = [
        pltpu.make_async_copy(iq_ref, iqall.at[chip, core], local.at[3]),
        pltpu.make_async_copy(q_ref, qall.at[chip], local.at[0]),
        pltpu.make_async_copy(k_ref, k_view(z, 0), local.at[1]),
    ]
    for copy in own:
        copy.start()

    pieces = sel_ref.shape[1] // 512

    def add_picks(i, total):
        at = pl.ds(pl.multiple_of((i % pieces) * 512, 512), 512)
        token = sel_ref[pl.ds(i // pieces, 1), at]
        to = (token >> 13) * 16 + ((token >> 4) & 15)
        window = (i // pieces) * 32 + ((token >> 8) & 31)
        value = ((token & 255) + 1).astype(F32)
        left = lax.broadcasted_iota(jnp.int32, (256, 512), 0) == to
        right = lax.broadcasted_iota(jnp.int32, (128, 512), 0) == window
        return total + lax.dot_general(
            jnp.where(left, 1.0, 0.0).astype(BF16),
            jnp.where(right, value, 0.0).astype(BF16),
            NT,
            preferred_element_type=F32,
        )

    table = lax.fori_loop(0, sel_ref.shape[0] * pieces, add_picks, jnp.zeros((256, 128), F32))
    tsend[...] = table.astype(BF16).reshape(16, 16, 128)

    table_copies = []

    def send_tables():
        for step in range(1, 16):
            to = (chip + step) % 16
            copy = remote(
                tsend.at[to], tall.at[chip], t_send.at[step], t_recv.at[step], {"ctx": to * 2 + core}
            )
            copy.start()
            table_copies.append(copy)
        own.append(pltpu.make_async_copy(tsend.at[chip], tall.at[chip], local.at[2]))
        own[-1].start()

    oa, ob = place(other)
    columns = (0, 3, 1, 2)

    def wait_partner(da, db):
        if db:
            j = columns.index(da)
            events = {3: ((5 + 4 * j, 0),), 1: ((6 + 4 * j, 0),), 2: ((7 + 4 * j, 1), (8 + 4 * j, 2))}[db]
        else:
            events = {0: ((0, 0),), 3: ((1, 0),), 1: ((2, 0),), 2: ((3, 1), (4, 2))}[da]
        for event, part in events:
            ref = iqall.at[chip_of(oa + da, ob + db, other), other, index_ring.halves[part]]
            remote(ref, ref, p_send.at[event], p_recv.at[event], partner).wait_recv()

    tile = 512
    tiles = keys_ref.shape[0] // tile

    def index_chip(p):
        for c in range(2):
            gates = iqall[p, c, 256:320, :].astype(F32)
            for r in range(4):
                gate_ref[pl.ds((c * 4 + r) * 64, 64), :] = jnp.broadcast_to(gates[:, r : r + 1], (64, 128))

        def token_tile(t):
            return pl.ds(pl.multiple_of(t * tile, tile), tile)

        def logits(t, slot):
            logit_ref[slot] = lax.dot_general(
                iqall[p, :, 0:256, :].reshape(512, 128), keys_ref[token_tile(t), :], NT, preferred_element_type=F32
            )

        def gated_sum(t, slot):
            columns = []
            for lanes in range(0, tile, 128):
                rows = []
                for i in range(8):
                    total = None
                    for h in range(0, 64, 8):
                        part = logit_ref[slot, i * 64 + h : i * 64 + h + 8, lanes : lanes + 128]
                        part = jnp.maximum(part, 0.0) * gate_ref[i * 64 + h : i * 64 + h + 8, :]
                        total = part if total is None else total + part
                    rows.append(jnp.sum(total, axis=0, keepdims=True))
                columns.append(jnp.concatenate(rows, axis=0))
            isc_ref[pl.ds(pl.multiple_of(p * 8, 8), 8), token_tile(t)] = jnp.concatenate(columns, axis=1)

        logits(0, 0)

        def two_tiles(i, carry):
            logits(i * 2 + 1, 1)
            gated_sum(i * 2, 0)
            logits(jnp.minimum(i * 2 + 2, tiles - 1), 0)
            gated_sum(i * 2 + 1, 1)
            return carry

        lax.fori_loop(0, tiles // 2, two_tiles, 0)

    def index_chips(low, high, dx, dy):
        def one(k, carry):
            index_chip((x + dx(k)) % 4 * 4 + (y + dy(k)) % 4)
            return carry

        lax.fori_loop(low, high, one, 0)

    beside = (lambda k: (1 - k // 2) * (1 + 2 * (k % 2)), lambda k: (k // 2) * (1 + 2 * (k % 2)))
    corner = (lambda k: 1 + 2 * (k % 2), lambda k: 1 + 2 * (k // 2))
    rest = (
        lambda k: 2 * (k == 0) + 2 * (k == 2) + 2 * (k == 3) + (k == 4) + 3 * (k == 5) + 2 * (k == 6),
        lambda k: 2 * (k == 1) + (k == 2) + 3 * (k == 3) + 2 * (k == 4) + 2 * (k == 5) + 2 * (k == 6),
    )

    index_ring.near()
    send_tables()
    index_ring.relay(0)
    index_ring.far()
    own[0].wait()
    keys_copy.wait()
    wait_partner(0, 0)
    index_chips(0, 1, lambda k: k, lambda k: k)
    index_ring.relay(1)
    index_ring.relay(2)
    index_ring.last(0)
    index_ring.relay(3)
    for j in (1, 2, 3):
        index_ring.last(j)
    query_ring.near()
    query_ring.relay(0)
    for da, db in ((3, 0), (1, 0), (0, 3), (0, 1)):
        wait_partner(da, db)
    index_chips(0, 4, *beside)
    query_ring.far()
    k_get(0, z + 3, 0)
    k_put(2, k_view(z + 3, 1), k_view(z + 3, 1), up)
    k_put(5, k_view(z + 3, 0), k_view(z + 3, 0), partner)
    k_get(1, z + 1, 0)
    k_put(3, k_view(z + 1, 2), k_view(z + 1, 2), down)
    k_put(6, k_view(z + 1, 0), k_view(z + 1, 0), partner)
    for da, db in ((3, 3), (3, 1), (1, 3), (1, 1)):
        wait_partner(da, db)
    index_chips(0, 2, *corner)
    query_ring.relay(1)
    query_ring.relay(2)
    index_chips(2, 4, *corner)
    for da, db in ((2, 0), (0, 2), (3, 2), (1, 2), (2, 3), (2, 1), (2, 2)):
        wait_partner(da, db)
    index_chips(0, 3, *rest)
    query_ring.relay(3)
    k_get(2, z + 2, 1)
    k_put(7, k_view(z + 2, 1), k_view(z + 2, 1), partner)
    k_get(3, z + 2, 2)
    k_put(8, k_view(z + 2, 2), k_view(z + 2, 2), partner)
    index_chips(3, 7, *rest)

    for j in range(4):
        query_ring.last(j)
    k_get(4, z, 0, other)
    k_get(5, z + 3, 0, other)
    k_get(6, z + 1, 0, other)
    k_get(7, z + 2, 1, other)
    k_get(8, z + 2, 2, other)
    for step in range(1, 16):
        frm = (chip + 16 - step) % 16
        remote(
            tall.at[frm], tall.at[frm], t_send.at[step], t_recv.at[step], partner
        ).wait_recv()
    for copy in own[1:]:
        copy.wait()
    query_ring.finish()
    index_ring.finish()
    for copy in to_partner + table_copies + k_sent:
        copy.wait_send()


def attend_kernel(
    qall, kall, tall, out_ref,
    kext, ksel, qbuf, rope, raw, picks, mlcol, mlin,
    s_opp, s_up, s_dn, r_opp0, r_opp1, r_up, r_dn,
    m_opp, m_up, m_dn, n_opp0, n_opp1, n_up, n_dn,
    acc, t_opp, t_up, t_dn, w_opp0, w_opp1, w_up, w_dn,
    e_opp, e_up, e_dn, f_opp0, f_opp1, f_up, f_dn,
    k_sem, q_sem, send, recv,
):
    ctx = lax.axis_index("ctx")
    core = ctx % 2
    u, v = place(core)
    up_u = {"ctx": chip_of(u + 1, v, core) * 2 + core}
    dn_u = {"ctx": chip_of(u + 3, v, core) * 2 + core}
    up_v = {"ctx": chip_of(u, v + 1, core) * 2 + core}
    dn_v = {"ctx": chip_of(u, v + 3, core) * 2 + core}
    order = (2, 1, 3, 0)

    barrier = pltpu.get_barrier_semaphore()
    for device in (up_u, dn_u, up_v, dn_v):
        pl.semaphore_signal(barrier, inc=1, device_id=device, device_id_type=MESH)

    def k_copy(w):
        at = pl.ds(pl.multiple_of((w % 4) * 256, 256), 256)
        return pltpu.make_async_copy(kall.at[w // 4, :, at], kext.at[w, pl.ds(0, 576), :], k_sem.at[w])

    groups = ((2, 2), (3, 1), (1, 3), (0, 0))

    def q_copies(group):
        copies = []
        for j in range(4):
            for half in range(2):
                chip = chip_of(u + groups[group][half], v + order[j], core)
                for r in (half * 2, half * 2 + 1):
                    copies.append((
                        qall.at[chip, :, pl.ds(r * 512, 512)],
                        qbuf.at[group % 2, j * 4 + r, pl.ds(0, 128), pl.ds(0, 512)],
                    ))
                copies.append((
                    qall.at[chip, :, pl.ds(2048 + half * 128, 128)],
                    rope.at[group % 2, j, :, pl.ds(half * 128, 128)],
                ))
        return [
            pltpu.make_async_copy(src, dst, q_sem.at[group % 2, n]) for n, (src, dst) in enumerate(copies)
        ]

    def start_k(w, carry):
        k_copy(w).start()
        return carry

    lax.fori_loop(0, 32, start_k, 0)
    for copy in q_copies(0):
        copy.start()

    ones = jnp.where(lax.broadcasted_iota(jnp.int32, (64, 256), 0) == 0, 1.0, 0.0).astype(BF16)

    def set_ones(w, carry):
        kext[w, pl.ds(576, 64), :] = ones
        return carry

    lax.fori_loop(0, 32, set_ones, 0)
    probe = jnp.where(lax.broadcasted_iota(jnp.int32, (16, 640), 1) == 576, 1.0, 0.0).astype(BF16)

    def set_probe(row, carry):
        for slot in range(2):
            qbuf[slot, row, pl.ds(128, 16), :] = probe
        return carry

    lax.fori_loop(0, 16, set_probe, 0)
    pl.semaphore_wait(barrier, 4)

    sent = []

    def put(k, src, dst, device):
        copy = remote(src, dst, send.at[k], recv.at[k], device)
        copy.start()
        sent.append(copy)

    def get(k, ref):
        remote(ref, ref, send.at[k], recv.at[k], up_u).wait_recv()

    lane = lax.broadcasted_iota(jnp.int32, (128, 128), 1)

    def column(ref, at):
        return jnp.sum(jnp.where(lane == at, ref[...], 0.0), axis=1, keepdims=True)

    def keep(ref, at, peak, total):
        ref[...] = jnp.where(lane == at, peak, jnp.where(lane == at + 1, total, ref[...]))

    def flip_in(slot, ref):
        rows = ref.shape[0]
        full = jnp.concatenate([ref[...], jnp.zeros((128 - rows, 128), F32)], axis=0)
        mlin[slot] = full.T

    def joined(one, two):
        sums1, peak1, total1 = one
        sums2, peak2, total2 = two
        peak = jnp.maximum(peak1, peak2)
        f1, f2 = jnp.exp2((peak1 - peak) * TO_LOG2), jnp.exp2((peak2 - peak) * TO_LOG2)
        return sums1 * f1 + sums2.astype(F32) * f2, peak, total1 * f1 + total2 * f2

    def gather_tokens(chunk):
        for j in range(4):
            for r in range(4):
                t = tall[chip_of(u + groups[chunk][r // 2], v + order[j], core)].astype(F32)
                moved = t if r == 0 else pltpu.roll(t, 128 - r * 32, axis=1)
                picks[pl.ds((j * 4 + r) * 16, 16), :] = moved
        wide = lax.broadcasted_iota(jnp.int32, (256, 128), 1)
        token = (lax.broadcasted_iota(jnp.int32, (256, 256), 1) + 1).astype(F32)

        def some_windows(i, carry):
            for step in range(4):
                w = i * 4 + step
                if chunk == 0:
                    k_copy(w).wait()
            for step in range(4):
                w = i * 4 + step
                want = jnp.sum(jnp.where(wide == w, picks[...], 0.0), axis=1, keepdims=True)
                onehot = jnp.where(token == want, 1.0, 0.0).astype(BF16)
                rows = lax.dot_general(onehot, kext[w], NT, preferred_element_type=F32)
                at = pl.ds(pl.multiple_of(w * 16, 16), 16)
                ksel[:, at, :] = rows.astype(BF16).reshape(16, 16, 640)
            return carry

        lax.fori_loop(0, 8, some_windows, 0)

    def set_rope(slot):
        def one_block(j, carry):
            for r in range(4):
                part = rope[slot, j, :, r * 64 : (r + 1) * 64]
                qbuf[slot, j * 4 + r, pl.ds(0, 128), pl.ds(512, 128)] = jnp.concatenate(
                    [part, jnp.zeros((128, 64), BF16)], axis=1
                )
            return carry

        lax.fori_loop(0, 4, one_block, 0)

    def score_row(slot, row, to):
        raw[to] = lax.dot_general(qbuf[slot, row], ksel[row], NT, preferred_element_type=F32)

    def attend_row(row, frm):
        scores = jnp.where(raw[frm, 128:129, :] > 0.5, raw[frm, 0:128, :], NONE)
        peak = jnp.maximum(jnp.max(scores, axis=1, keepdims=True), FLOOR)
        weights = jnp.exp2((scores - peak) * TO_LOG2)
        total = jnp.sum(weights, axis=1, keepdims=True)
        sums = jnp.dot(weights.astype(BF16), ksel[row, :, 0:512], preferred_element_type=F32)
        return sums, peak, total

    def half_chunk(chunk, half, put_row, merges):
        slot = chunk % 2
        score_row(slot, half * 2, 0)

        def one_block(j, carry):
            for r2 in range(2):
                row = j * 4 + half * 2 + r2
                score_row(slot, (row + 1 if r2 == 0 else jnp.minimum(row + 3, 12 + half * 2)), 1 - r2)
                got = attend_row(row, r2)
                for at_slot, ref in merges:
                    at = j * 4 + r2 * 2
                    got = joined(
                        got, (ref[j, r2], column(mlin.at[at_slot], at), column(mlin.at[at_slot], at + 1))
                    )
                put_row(j, r2, *got)
            return carry

        lax.fori_loop(0, 4, one_block, 0)

    def send_half(chunk, half, sums_ref, ml_ref, merges):
        def put_row(j, r2, sums, peak, total):
            sums_ref[half, j, r2] = sums.astype(BF16)
            keep(mlcol, j * 4 + r2 * 2, peak, total)

        half_chunk(chunk, half, put_row, merges)
        ml_ref[half] = mlcol[...].T[0:16]

    mlcol[...] = jnp.zeros((128, 128), F32)

    def next_chunk(chunk):
        for copy in q_copies(chunk):
            copy.wait()
        if chunk < 3:
            for copy in q_copies(chunk + 1):
                copy.start()
        set_rope(chunk % 2)
        gather_tokens(chunk)

    next_chunk(0)
    send_half(0, 0, s_opp, m_opp, ())
    put(0, s_opp.at[0], r_opp0, up_u)
    put(1, m_opp.at[0], n_opp0, up_u)
    send_half(0, 1, s_opp, m_opp, ())
    put(2, s_opp.at[1], r_opp1, dn_u)
    put(3, m_opp.at[1], n_opp1, dn_u)

    next_chunk(1)
    send_half(1, 1, s_up, m_up, ())
    put(4, s_up.at[1], r_up.at[1], up_u)
    put(5, m_up.at[1], n_up.at[1], up_u)
    send_half(1, 0, s_dn, m_dn, ())
    put(8, s_dn.at[0], r_dn.at[0], dn_u)
    put(9, m_dn.at[0], n_dn.at[0], dn_u)

    next_chunk(2)
    get(0, r_opp0)
    get(1, n_opp0)
    flip_in(0, n_opp0)
    send_half(2, 0, s_up, m_up, ((0, r_opp0),))
    put(6, s_up.at[0], r_up.at[0], up_u)
    put(7, m_up.at[0], n_up.at[0], up_u)
    get(2, r_opp1)
    get(3, n_opp1)
    flip_in(0, n_opp1)
    send_half(2, 1, s_dn, m_dn, ((0, r_opp1),))
    put(10, s_dn.at[1], r_dn.at[1], dn_u)
    put(11, m_dn.at[1], n_dn.at[1], dn_u)

    next_chunk(3)
    for half, early, early_ml, k in ((0, r_dn, n_dn, 8), (1, r_up, n_up, 4)):
        get(k, early.at[half])
        get(k + 1, early_ml.at[half])
        flip_in(0, early_ml.at[half])

        def put_row(j, r2, sums, peak, total):
            acc[j, half * 2 + r2] = sums
            keep(mlcol, j * 8 + half * 4 + r2 * 2, peak, total)

        half_chunk(3, half, put_row, ((0, early.at[half]),))

    get(6, r_up.at[0])
    get(7, n_up.at[0])
    flip_in(0, n_up.at[0])
    get(10, r_dn.at[1])
    get(11, n_dn.at[1])
    flip_in(1, n_dn.at[1])

    def add_late(j):
        for r in range(4):
            half, r2 = r // 2, r % 2
            at, here = j * 4 + r2 * 2, j * 8 + r * 2
            late = (r_up, r_dn)[half][half, j, r2]
            got = (acc[j, r], column(mlcol, here), column(mlcol, here + 1))
            got = joined(got, (late, column(mlin.at[half], at), column(mlin.at[half], at + 1)))
            acc[j, r] = got[0]
            keep(mlcol, here, got[1], got[2])

    def second_send(j, half, sums_ref, ml_ref, merge=None):
        if merge is not None:
            flip_in(2, merge[1])
        for r2 in range(2):
            r = half * 2 + r2
            at = j * 8 + r * 2
            if merge is None:
                sums_ref[half, r2] = acc[j, r].astype(BF16)
                continue
            got = (acc[j, r], column(mlcol, at), column(mlcol, at + 1))
            got = joined(got, (merge[0][r2], column(mlin.at[2], at % 8), column(mlin.at[2], at % 8 + 1)))
            keep(mlcol, at, got[1], got[2])
            sums_ref[half, r2] = got[0].astype(BF16)
        ml_ref[half] = mlcol[...].T[j * 8 : j * 8 + 8]

    add_late(0)
    second_send(0, 0, t_opp, e_opp)
    put(12, t_opp.at[0], w_opp0, up_v)
    put(13, e_opp.at[0], f_opp0, up_v)
    second_send(0, 1, t_opp, e_opp)
    put(14, t_opp.at[1], w_opp1, dn_v)
    put(15, e_opp.at[1], f_opp1, dn_v)
    add_late(1)
    second_send(1, 1, t_up, e_up)
    put(16, t_up.at[1], w_up.at[1], up_v)
    put(17, e_up.at[1], f_up.at[1], up_v)
    add_late(2)
    second_send(2, 0, t_dn, e_dn)
    put(20, t_dn.at[0], w_dn.at[0], dn_v)
    put(21, e_dn.at[0], f_dn.at[0], dn_v)
    get(12, w_opp0)
    get(13, f_opp0)
    second_send(1, 0, t_up, e_up, (w_opp0, f_opp0))
    put(18, t_up.at[0], w_up.at[0], up_v)
    put(19, e_up.at[0], f_up.at[0], up_v)
    get(14, w_opp1)
    get(15, f_opp1)
    second_send(2, 1, t_dn, e_dn, (w_opp1, f_opp1))
    put(22, t_dn.at[1], w_dn.at[1], dn_v)
    put(23, e_dn.at[1], f_dn.at[1], dn_v)
    add_late(3)

    for half in (1, 0):
        get(16 if half else 18, w_up.at[half])
        get(17 if half else 19, f_up.at[half])
        get(22 if half else 20, w_dn.at[half])
        get(23 if half else 21, f_dn.at[half])
        flip_in(half * 2, f_up.at[half])
        flip_in(half * 2 + 1, f_dn.at[half])
    for r in range(4):
        half, r2 = r // 2, r % 2
        at = 24 + r * 2
        got = (acc[3, r], column(mlcol, at), column(mlcol, at + 1))
        for slot, ref in ((half * 2, w_up), (half * 2 + 1, w_dn)):
            got = joined(got, (ref[half, r2], column(mlin.at[slot], r * 2), column(mlin.at[slot], r * 2 + 1)))
        out_ref[r] = (got[0] / got[2]).astype(BF16)
    for copy in sent:
        copy.wait_send()


def vmem():
    return pl.BlockSpec(memory_space=pltpu.VMEM)


def anywhere():
    return pl.BlockSpec(memory_space=pl.ANY)


def body(latent_cache, index_keys, query_latent, index_query, index_gates, selected):
    rows, heads, width = query_latent.shape
    tokens = latent_cache.shape[0]
    kt = latent_cache.T
    q_latent = query_latent[:, :, :LATENT].transpose(1, 0, 2).reshape(heads, rows * LATENT)
    q_rope = query_latent[:, :, LATENT:].transpose(1, 0, 2).reshape(heads, rows * (width - LATENT))
    qw = jnp.concatenate([q_latent, q_rope], axis=1)
    gates = jnp.pad(index_gates.T, ((0, 0), (0, 128 - rows)))
    iqg = jnp.concatenate([index_query.reshape(-1, 128), gates], axis=0)
    dma = pltpu.SemaphoreType.DMA

    qall, kall, tall, index_scores = pl.pallas_call(
        gather_kernel,
        out_shape=(
            jax.ShapeDtypeStruct((16,) + qw.shape, BF16),
            jax.ShapeDtypeStruct((8, width, tokens), BF16),
            jax.ShapeDtypeStruct((16, 16, 128), BF16),
            jax.ShapeDtypeStruct((rows * 32, index_keys.shape[0]), F32),
        ),
        in_specs=[vmem(), vmem(), vmem(), anywhere(), vmem()],
        out_specs=(anywhere(), anywhere(), anywhere(), vmem()),
        scratch_shapes=[
            pltpu.VMEM((16, 2) + iqg.shape, BF16),
            pltpu.VMEM((16, 16, 128), BF16),
            pltpu.VMEM((512, 128), F32),
            pltpu.VMEM(index_keys.shape, BF16),
            pltpu.VMEM((2, 512, 512), F32),
            dma((20,)), dma((20,)), dma((20,)), dma((20,)), dma((21,)), dma((21,)),
            dma((9,)), dma((9,)), dma((16,)), dma((16,)), dma((5,)),
        ],
        compiler_params=pltpu.CompilerParams(
            collective_id=0, has_side_effects=True, vmem_limit_bytes=48 * 1024 * 1024
        ),
        name="gather",
    )(qw, kt, iqg, index_keys, selected)

    half = (4, 2, heads, LATENT)
    quarter = (2, heads, LATENT)
    attended = pl.pallas_call(
        attend_kernel,
        out_shape=jax.ShapeDtypeStruct((rows, heads, LATENT), BF16),
        in_specs=[anywhere(), anywhere(), vmem()],
        out_specs=vmem(),
        scratch_shapes=[
            pltpu.VMEM((32, 640, 256), BF16),
            pltpu.VMEM((16, 512, 640), BF16),
            pltpu.VMEM((2, 16, 144, 640), BF16),
            pltpu.VMEM((2, 4, heads, 256), BF16),
            pltpu.VMEM((2, 144, 512), F32),
            pltpu.VMEM((256, 128), F32),
            pltpu.VMEM((128, 128), F32),
            pltpu.VMEM((4, 128, 128), F32),
        ]
        + [pltpu.VMEM((2,) + half, BF16)] * 3
        + [pltpu.VMEM(half, BF16)] * 2
        + [pltpu.VMEM((2,) + half, BF16)] * 2
        + [pltpu.VMEM((2, 16, 128), F32)] * 3
        + [pltpu.VMEM((16, 128), F32)] * 2
        + [pltpu.VMEM((2, 16, 128), F32)] * 2
        + [pltpu.VMEM((4, rows, heads, LATENT), F32)]
        + [pltpu.VMEM((2,) + quarter, BF16)] * 3
        + [pltpu.VMEM(quarter, BF16)] * 2
        + [pltpu.VMEM((2,) + quarter, BF16)] * 2
        + [pltpu.VMEM((2, 8, 128), F32)] * 3
        + [pltpu.VMEM((8, 128), F32)] * 2
        + [pltpu.VMEM((2, 8, 128), F32)] * 2
        + [dma((32,)), dma((2, 24)), dma((24,)), dma((24,))],
        compiler_params=pltpu.CompilerParams(
            collective_id=1, has_side_effects=True, vmem_limit_bytes=60 * 1024 * 1024
        ),
        name="attend",
    )(qall, kall, tall)
    return attended, index_scores


def solution(mesh):
    return jax.shard_map(
        body,
        mesh=mesh,
        in_specs=(
            P(("ctx", "row"), None),
            P("ctx", None),
            P(("row", "ctx"), None, None),
            P(("row", "ctx"), None, None),
            P(("row", "ctx"), None),
            P(("row", "ctx"), None),
        ),
        out_specs=(P(("row", "ctx"), None, None), P("row", "ctx")),
        check_vma=False,
    )
```

```python
import math

import jax
import jax.numpy as jnp
from jax import lax
from jax.experimental import pallas as pl
from jax.experimental.pallas import tpu as pltpu
from jax.sharding import PartitionSpec as P

MESH = pl.DeviceIdType.MESH
LATENT = 512
TO_LOG2 = 192 ** (-0.5) * math.log2(math.e)
NONE = -1e30
FLOOR = -1e29
F32 = jnp.float32
BF16 = jnp.bfloat16
NT = (((1,), (1,)), ((), ()))


def remote(src, dst, send, recv, device):
    return pltpu.make_async_remote_copy(
        src_ref=src, dst_ref=dst, send_sem=send, recv_sem=recv, device_id=device, device_id_type=MESH
    )


def place(core):
    chip = lax.axis_index("ctx") // 2
    x, y = chip // 4, chip % 4
    return x * (1 - core) + y * core, y * (1 - core) + x * core


def chip_of(a, b, core):
    a, b = a % 4, b % 4
    return (a * (1 - core) + b * core) * 4 + b * (1 - core) + a * core


class Ring:
    def __init__(self, own, buf, rows, send, recv, core, on_block=None):
        self.own, self.buf, self.send, self.recv, self.core = own, buf, send, recv, core
        self.halves = (pl.ds(0, rows), pl.ds(0, rows // 2), pl.ds(rows // 2, rows // 2))
        self.a, self.b = place(core)
        self.columns = (self.a, self.a + 3, self.a + 1, self.a + 2)
        self.sent = []
        self.on_block = on_block

    def view(self, a, b, part):
        return self.buf(chip_of(a, b, self.core), self.halves[part])

    def put(self, k, block, part, to, own=False):
        src = self.own if own else self.view(*block, part)
        device = {"ctx": chip_of(*to, self.core) * 2 + self.core}
        copy = remote(src, self.view(*block, part), self.send.at[k], self.recv.at[k], device)
        copy.start()
        self.sent.append(copy)

    def get(self, k, block, part, event):
        ref = self.view(*block, part)
        remote(ref, ref, self.send.at[k], self.recv.at[k], {"ctx": lax.axis_index("ctx")}).wait_recv()
        if self.on_block is not None:
            self.on_block(event, block, part)

    def start(self):
        a, b = self.a, self.b
        self.put(4, (a, b), 0, (a, b + 1), own=True)
        self.put(5, (a, b), 0, (a, b + 3), own=True)
        self.put(0, (a, b), 0, (a + 1, b), own=True)
        self.put(1, (a, b), 0, (a + 3, b), own=True)

    def second(self, j):
        block = (self.columns[j], self.b)
        self.put(4 + 4 * j, block, 0, (self.a, self.b + 1))
        self.put(5 + 4 * j, block, 0, (self.a, self.b + 3))

    def near(self):
        a, b = self.a, self.b
        self.get(0, (a + 3, b), 0, 1)
        self.put(2, (a + 3, b), 1, (a + 1, b))
        self.second(1)
        self.get(1, (a + 1, b), 0, 2)
        self.put(3, (a + 1, b), 2, (a + 3, b))
        self.second(2)

    def far(self):
        a, b = self.a, self.b
        self.get(2, (a + 2, b), 1, 3)
        self.get(3, (a + 2, b), 2, 4)
        self.second(3)

    def relay(self, j):
        column, b = self.columns[j], self.b
        self.get(4 + 4 * j, (column, b + 3), 0, 5 + 4 * j)
        self.put(6 + 4 * j, (column, b + 3), 1, (self.a, b + 1))
        self.get(5 + 4 * j, (column, b + 1), 0, 6 + 4 * j)
        self.put(7 + 4 * j, (column, b + 1), 2, (self.a, b + 3))

    def last(self, j):
        column, b = self.columns[j], self.b
        self.get(6 + 4 * j, (column, b + 2), 1, 7 + 4 * j)
        self.get(7 + 4 * j, (column, b + 2), 2, 8 + 4 * j)

    def finish(self):
        for copy in self.sent:
            copy.wait_send()


def kernel(
    q_ref, k_ref, iq_ref, keys_hbm, sel_ref,
    qall, isc_ref, out_ref,
    kext, tall, iqall, tsend, gate_ref, keys_ref, logit_ref,
    q_send, q_recv, i_send, i_recv, p_send, p_recv, k_send, k_recv, t_send, t_recv, local,
    *attend_refs,
):
    ctx, z = lax.axis_index("ctx"), lax.axis_index("row")
    core, chip = ctx % 2, ctx // 2
    other = 1 - core
    partner = {"ctx": chip * 2 + other}
    x, y = chip // 4, chip % 4

    keys_copy = pltpu.make_async_copy(keys_hbm, keys_ref, local.at[4])
    keys_copy.start()
    ones = jnp.where(lax.broadcasted_iota(jnp.int32, (64, 1024), 0) == 0, 1.0, 0.0).astype(BF16)

    def set_ones(block, carry):
        kext[block, pl.ds(576, 64), :] = ones
        return carry

    lax.fori_loop(0, 8, set_ones, 0)
    barrier = pltpu.get_barrier_semaphore()
    for step in range(1, 16):
        pl.semaphore_signal(
            barrier, inc=1, device_id={"ctx": ((chip + step) % 16) * 2 + core}, device_id_type=MESH
        )
    pl.semaphore_signal(barrier, inc=1, device_id=partner, device_id_type=MESH)
    for step in (1, 3):
        pl.semaphore_signal(barrier, inc=1, device_id={"row": (z + step) % 4}, device_id_type=MESH)
    pl.semaphore_wait(barrier, 18)

    to_partner = []

    def hand_on(event, block, part):
        ref = index_ring.view(*block, part)
        copy = remote(ref, ref, p_send.at[event], p_recv.at[event], partner)
        copy.start()
        to_partner.append(copy)

    index_ring = Ring(
        iq_ref, lambda p, rows: iqall.at[p, core, rows], iq_ref.shape[0], i_send, i_recv, core, hand_on
    )
    index_ring.start()
    copy = remote(iq_ref, iqall.at[chip, core], p_send.at[0], p_recv.at[0], partner)
    copy.start()
    to_partner.append(copy)

    k_rows = k_ref.shape[0]
    parts = (pl.ds(0, k_rows), pl.ds(0, k_rows // 2), pl.ds(k_rows // 2, k_rows // 2))
    k_sent = []

    def k_view(depth, part, c=core):
        return kext.at[c * 4 + depth % 4, parts[part]]

    def k_put(k, src, dst, device):
        copy = remote(src, dst, k_send.at[k], k_recv.at[k], device)
        copy.start()
        k_sent.append(copy)

    def k_get(k, depth, part, c=core):
        ref = k_view(depth, part, c)
        remote(ref, ref, k_send.at[k], k_recv.at[k], {"row": z}).wait_recv()

    up, down = {"row": (z + 1) % 4}, {"row": (z + 3) % 4}
    query_ring = Ring(q_ref, lambda p, rows: qall.at[p, rows], q_ref.shape[0], q_send, q_recv, core)
    query_ring.start()
    k_put(0, k_ref, k_view(z, 0), up)
    k_put(1, k_ref, k_view(z, 0), down)
    k_put(4, k_ref, k_view(z, 0), partner)

    own = [
        pltpu.make_async_copy(iq_ref, iqall.at[chip, core], local.at[3]),
        pltpu.make_async_copy(q_ref, qall.at[chip], local.at[0]),
        pltpu.make_async_copy(k_ref, k_view(z, 0), local.at[1]),
    ]
    for copy in own:
        copy.start()

    pieces = sel_ref.shape[1] // 512

    def add_picks(i, total):
        at = pl.ds(pl.multiple_of((i % pieces) * 512, 512), 512)
        token = sel_ref[pl.ds(i // pieces, 1), at]
        to = (token >> 13) * 16 + ((token >> 4) & 15)
        window = (i // pieces) * 32 + ((token >> 8) & 31)
        value = ((token & 255) + 1).astype(F32)
        left = lax.broadcasted_iota(jnp.int32, (256, 512), 0) == to
        right = lax.broadcasted_iota(jnp.int32, (128, 512), 0) == window
        return total + lax.dot_general(
            jnp.where(left, 1.0, 0.0).astype(BF16),
            jnp.where(right, value, 0.0).astype(BF16),
            NT,
            preferred_element_type=F32,
        )

    table = lax.fori_loop(0, sel_ref.shape[0] * pieces, add_picks, jnp.zeros((256, 128), F32))
    tsend[...] = table.astype(BF16).reshape(16, 16, 128)

    table_copies = []

    def send_tables():
        for step in range(1, 16):
            to = (chip + step) % 16
            copy = remote(
                tsend.at[to], tall.at[chip], t_send.at[step], t_recv.at[step], {"ctx": to * 2 + core}
            )
            copy.start()
            table_copies.append(copy)
        own.append(pltpu.make_async_copy(tsend.at[chip], tall.at[chip], local.at[2]))
        own[-1].start()

    oa, ob = place(other)
    columns = (0, 3, 1, 2)

    def wait_partner(da, db):
        if db:
            j = columns.index(da)
            events = {3: ((5 + 4 * j, 0),), 1: ((6 + 4 * j, 0),), 2: ((7 + 4 * j, 1), (8 + 4 * j, 2))}[db]
        else:
            events = {0: ((0, 0),), 3: ((1, 0),), 1: ((2, 0),), 2: ((3, 1), (4, 2))}[da]
        for event, part in events:
            ref = iqall.at[chip_of(oa + da, ob + db, other), other, index_ring.halves[part]]
            remote(ref, ref, p_send.at[event], p_recv.at[event], partner).wait_recv()

    tile = 512
    tiles = keys_ref.shape[0] // tile

    def index_chip(p):
        for c in range(2):
            gates = iqall[p, c, 256:320, :].astype(F32)
            for r in range(4):
                gate_ref[pl.ds((c * 4 + r) * 64, 64), :] = jnp.broadcast_to(gates[:, r : r + 1], (64, 128))

        def token_tile(t):
            return pl.ds(pl.multiple_of(t * tile, tile), tile)

        def logits(t, slot):
            logit_ref[slot] = lax.dot_general(
                iqall[p, :, 0:256, :].reshape(512, 128), keys_ref[token_tile(t), :], NT, preferred_element_type=F32
            )

        def gated_sum(t, slot):
            columns = []
            for lanes in range(0, tile, 128):
                rows = []
                for i in range(8):
                    total = None
                    for h in range(0, 64, 8):
                        part = logit_ref[slot, i * 64 + h : i * 64 + h + 8, lanes : lanes + 128]
                        part = jnp.maximum(part, 0.0) * gate_ref[i * 64 + h : i * 64 + h + 8, :]
                        total = part if total is None else total + part
                    rows.append(jnp.sum(total, axis=0, keepdims=True))
                columns.append(jnp.concatenate(rows, axis=0))
            isc_ref[pl.ds(pl.multiple_of(p * 8, 8), 8), token_tile(t)] = jnp.concatenate(columns, axis=1)

        logits(0, 0)

        def two_tiles(i, carry):
            logits(i * 2 + 1, 1)
            gated_sum(i * 2, 0)
            logits(jnp.minimum(i * 2 + 2, tiles - 1), 0)
            gated_sum(i * 2 + 1, 1)
            return carry

        lax.fori_loop(0, tiles // 2, two_tiles, 0)

    def index_chips(low, high, dx, dy):
        def one(k, carry):
            index_chip((x + dx(k)) % 4 * 4 + (y + dy(k)) % 4)
            return carry

        lax.fori_loop(low, high, one, 0)

    beside = (lambda k: (1 - k // 2) * (1 + 2 * (k % 2)), lambda k: (k // 2) * (1 + 2 * (k % 2)))
    corner = (lambda k: 1 + 2 * (k % 2), lambda k: 1 + 2 * (k // 2))
    rest = (
        lambda k: 2 * (k == 0) + 2 * (k == 2) + 2 * (k == 3) + (k == 4) + 3 * (k == 5) + 2 * (k == 6),
        lambda k: 2 * (k == 1) + (k == 2) + 3 * (k == 3) + 2 * (k == 4) + 2 * (k == 5) + 2 * (k == 6),
    )

    index_ring.near()
    send_tables()
    index_ring.relay(0)
    index_ring.far()
    own[0].wait()
    keys_copy.wait()
    wait_partner(0, 0)
    index_chips(0, 1, lambda k: k, lambda k: k)
    index_ring.relay(1)
    index_ring.relay(2)
    index_ring.last(0)
    index_ring.relay(3)
    for j in (1, 2, 3):
        index_ring.last(j)
    query_ring.near()
    query_ring.relay(0)
    for da, db in ((3, 0), (1, 0), (0, 3), (0, 1)):
        wait_partner(da, db)
    index_chips(0, 4, *beside)
    query_ring.far()
    k_get(0, z + 3, 0)
    k_put(2, k_view(z + 3, 1), k_view(z + 3, 1), up)
    k_put(5, k_view(z + 3, 0), k_view(z + 3, 0), partner)
    k_get(1, z + 1, 0)
    k_put(3, k_view(z + 1, 2), k_view(z + 1, 2), down)
    k_put(6, k_view(z + 1, 0), k_view(z + 1, 0), partner)
    for da, db in ((3, 3), (3, 1), (1, 3), (1, 1)):
        wait_partner(da, db)
    index_chips(0, 2, *corner)
    query_ring.relay(1)
    query_ring.relay(2)
    index_chips(2, 4, *corner)
    for da, db in ((2, 0), (0, 2), (3, 2), (1, 2), (2, 3), (2, 1), (2, 2)):
        wait_partner(da, db)
    index_chips(0, 3, *rest)
    query_ring.relay(3)
    k_get(2, z + 2, 1)
    k_put(7, k_view(z + 2, 1), k_view(z + 2, 1), partner)
    k_get(3, z + 2, 2)
    k_put(8, k_view(z + 2, 2), k_view(z + 2, 2), partner)
    index_chips(3, 7, *rest)

    k_get(4, z, 0, other)
    k_get(5, z + 3, 0, other)
    k_get(6, z + 1, 0, other)
    k_get(7, z + 2, 1, other)
    k_get(8, z + 2, 2, other)
    for step in range(1, 16):
        frm = (chip + 16 - step) % 16
        remote(
            tall.at[frm], tall.at[frm], t_send.at[step], t_recv.at[step], partner
        ).wait_recv()
    for copy in own[1:]:
        copy.wait()

    def queries_here():
        for j in range(4):
            query_ring.last(j)

    attend(qall, kext, tall, out_ref, queries_here, *attend_refs)
    query_ring.finish()
    index_ring.finish()
    for copy in to_partner + table_copies + k_sent:
        copy.wait_send()


def attend(
    qall, kext, tall, out_ref, queries_here,
    ksel, qbuf, rope, raw, picks, mlcol, mlin,
    s_opp, s_up, s_dn, r_opp0, r_opp1, r_up, r_dn,
    m_opp, m_up, m_dn, n_opp0, n_opp1, n_up, n_dn,
    acc, t_opp, t_up, t_dn, w_opp0, w_opp1, w_up, w_dn,
    e_opp, e_up, e_dn, f_opp0, f_opp1, f_up, f_dn,
    q_sem, send, recv,
):
    ctx = lax.axis_index("ctx")
    core = ctx % 2
    u, v = place(core)
    up_u = {"ctx": chip_of(u + 1, v, core) * 2 + core}
    dn_u = {"ctx": chip_of(u + 3, v, core) * 2 + core}
    up_v = {"ctx": chip_of(u, v + 1, core) * 2 + core}
    dn_v = {"ctx": chip_of(u, v + 3, core) * 2 + core}
    order = (2, 1, 3, 0)

    groups = ((2, 2), (3, 1), (1, 3), (0, 0))

    def q_copies(group):
        copies = []
        for j in range(4):
            for half in range(2):
                chip = chip_of(u + groups[group][half], v + order[j], core)
                for r in (half * 2, half * 2 + 1):
                    copies.append((
                        qall.at[chip, :, pl.ds(r * 512, 512)],
                        qbuf.at[group % 2, j * 4 + r, pl.ds(0, 128), pl.ds(0, 512)],
                    ))
                copies.append((
                    qall.at[chip, :, pl.ds(2048 + half * 128, 128)],
                    rope.at[group % 2, j, :, pl.ds(half * 128, 128)],
                ))
        return [
            pltpu.make_async_copy(src, dst, q_sem.at[group % 2, n]) for n, (src, dst) in enumerate(copies)
        ]

    probe = jnp.where(lax.broadcasted_iota(jnp.int32, (16, 640), 1) == 576, 1.0, 0.0).astype(BF16)

    def set_probe(row, carry):
        for slot in range(2):
            qbuf[slot, row, pl.ds(128, 16), :] = probe
        return carry

    lax.fori_loop(0, 16, set_probe, 0)
    sent = []

    def put(k, src, dst, device):
        copy = remote(src, dst, send.at[k], recv.at[k], device)
        copy.start()
        sent.append(copy)

    def get(k, ref):
        remote(ref, ref, send.at[k], recv.at[k], up_u).wait_recv()

    lane = lax.broadcasted_iota(jnp.int32, (128, 128), 1)

    def column(ref, at):
        return jnp.sum(jnp.where(lane == at, ref[...], 0.0), axis=1, keepdims=True)

    def keep(ref, at, peak, total):
        ref[...] = jnp.where(lane == at, peak, jnp.where(lane == at + 1, total, ref[...]))

    def flip_in(slot, ref):
        rows = ref.shape[0]
        full = jnp.concatenate([ref[...], jnp.zeros((128 - rows, 128), F32)], axis=0)
        mlin[slot] = full.T

    def joined(one, two):
        sums1, peak1, total1 = one
        sums2, peak2, total2 = two
        peak = jnp.maximum(peak1, peak2)
        f1, f2 = jnp.exp2((peak1 - peak) * TO_LOG2), jnp.exp2((peak2 - peak) * TO_LOG2)
        return sums1 * f1 + sums2.astype(F32) * f2, peak, total1 * f1 + total2 * f2

    def gather_tokens(chunk):
        for j in range(4):
            for r in range(4):
                t = tall[chip_of(u + groups[chunk][r // 2], v + order[j], core)].astype(F32)
                moved = t if r == 0 else pltpu.roll(t, 128 - r * 32, axis=1)
                picks[pl.ds((j * 4 + r) * 16, 16), :] = moved
        wide = lax.broadcasted_iota(jnp.int32, (256, 128), 1)
        token = (lax.broadcasted_iota(jnp.int32, (256, 256), 1) + 1).astype(F32)

        def some_windows(i, carry):
            for step in range(4):
                w = i * 4 + step
                want = jnp.sum(jnp.where(wide == w, picks[...], 0.0), axis=1, keepdims=True)
                onehot = jnp.where(token == want, 1.0, 0.0).astype(BF16)
                rows = lax.dot_general(
                    onehot, kext[i, :, step * 256 : (step + 1) * 256], NT, preferred_element_type=F32
                )
                at = pl.ds(pl.multiple_of(w * 16, 16), 16)
                ksel[:, at, :] = rows.astype(BF16).reshape(16, 16, 640)
            return carry

        lax.fori_loop(0, 8, some_windows, 0)

    def set_rope(slot):
        def one_block(j, carry):
            for r in range(4):
                part = rope[slot, j, :, r * 64 : (r + 1) * 64]
                qbuf[slot, j * 4 + r, pl.ds(0, 128), pl.ds(512, 128)] = jnp.concatenate(
                    [part, jnp.zeros((128, 64), BF16)], axis=1
                )
            return carry

        lax.fori_loop(0, 4, one_block, 0)

    def score_row(slot, row, to):
        raw[to] = lax.dot_general(qbuf[slot, row], ksel[row], NT, preferred_element_type=F32)

    def attend_row(row, frm):
        scores = jnp.where(raw[frm, 128:129, :] > 0.5, raw[frm, 0:128, :], NONE)
        peak = jnp.maximum(jnp.max(scores, axis=1, keepdims=True), FLOOR)
        weights = jnp.exp2((scores - peak) * TO_LOG2)
        total = jnp.sum(weights, axis=1, keepdims=True)
        sums = jnp.dot(weights.astype(BF16), ksel[row, :, 0:512], preferred_element_type=F32)
        return sums, peak, total

    def half_chunk(chunk, half, put_row, merges):
        slot = chunk % 2
        score_row(slot, half * 2, 0)

        def one_block(j, carry):
            for r2 in range(2):
                row = j * 4 + half * 2 + r2
                score_row(slot, (row + 1 if r2 == 0 else jnp.minimum(row + 3, 12 + half * 2)), 1 - r2)
                got = attend_row(row, r2)
                for at_slot, ref in merges:
                    at = j * 4 + r2 * 2
                    got = joined(
                        got, (ref[j, r2], column(mlin.at[at_slot], at), column(mlin.at[at_slot], at + 1))
                    )
                put_row(j, r2, *got)
            return carry

        lax.fori_loop(0, 4, one_block, 0)

    def send_half(chunk, half, sums_ref, ml_ref, merges):
        def put_row(j, r2, sums, peak, total):
            sums_ref[half, j, r2] = sums.astype(BF16)
            keep(mlcol, j * 4 + r2 * 2, peak, total)

        half_chunk(chunk, half, put_row, merges)
        ml_ref[half] = mlcol[...].T[0:16]

    mlcol[...] = jnp.zeros((128, 128), F32)

    def next_chunk(chunk):
        if chunk == 0:
            gather_tokens(chunk)
            queries_here()
            for copy in q_copies(chunk):
                copy.start()
        for copy in q_copies(chunk):
            copy.wait()
        if chunk < 3:
            for copy in q_copies(chunk + 1):
                copy.start()
        set_rope(chunk % 2)
        if chunk:
            gather_tokens(chunk)

    next_chunk(0)
    send_half(0, 0, s_opp, m_opp, ())
    put(0, s_opp.at[0], r_opp0, up_u)
    put(1, m_opp.at[0], n_opp0, up_u)
    send_half(0, 1, s_opp, m_opp, ())
    put(2, s_opp.at[1], r_opp1, dn_u)
    put(3, m_opp.at[1], n_opp1, dn_u)

    next_chunk(1)
    send_half(1, 1, s_up, m_up, ())
    put(4, s_up.at[1], r_up.at[1], up_u)
    put(5, m_up.at[1], n_up.at[1], up_u)
    send_half(1, 0, s_dn, m_dn, ())
    put(8, s_dn.at[0], r_dn.at[0], dn_u)
    put(9, m_dn.at[0], n_dn.at[0], dn_u)

    next_chunk(2)
    get(0, r_opp0)
    get(1, n_opp0)
    flip_in(0, n_opp0)
    send_half(2, 0, s_up, m_up, ((0, r_opp0),))
    put(6, s_up.at[0], r_up.at[0], up_u)
    put(7, m_up.at[0], n_up.at[0], up_u)
    get(2, r_opp1)
    get(3, n_opp1)
    flip_in(0, n_opp1)
    send_half(2, 1, s_dn, m_dn, ((0, r_opp1),))
    put(10, s_dn.at[1], r_dn.at[1], dn_u)
    put(11, m_dn.at[1], n_dn.at[1], dn_u)

    next_chunk(3)
    for half, early, early_ml, k in ((0, r_dn, n_dn, 8), (1, r_up, n_up, 4)):
        get(k, early.at[half])
        get(k + 1, early_ml.at[half])
        flip_in(0, early_ml.at[half])

        def put_row(j, r2, sums, peak, total):
            acc[j, half * 2 + r2] = sums
            keep(mlcol, j * 8 + half * 4 + r2 * 2, peak, total)

        half_chunk(3, half, put_row, ((0, early.at[half]),))

    get(6, r_up.at[0])
    get(7, n_up.at[0])
    flip_in(0, n_up.at[0])
    get(10, r_dn.at[1])
    get(11, n_dn.at[1])
    flip_in(1, n_dn.at[1])

    def add_late(j):
        for r in range(4):
            half, r2 = r // 2, r % 2
            at, here = j * 4 + r2 * 2, j * 8 + r * 2
            late = (r_up, r_dn)[half][half, j, r2]
            got = (acc[j, r], column(mlcol, here), column(mlcol, here + 1))
            got = joined(got, (late, column(mlin.at[half], at), column(mlin.at[half], at + 1)))
            acc[j, r] = got[0]
            keep(mlcol, here, got[1], got[2])

    def second_send(j, half, sums_ref, ml_ref, merge=None):
        if merge is not None:
            flip_in(2, merge[1])
        for r2 in range(2):
            r = half * 2 + r2
            at = j * 8 + r * 2
            if merge is None:
                sums_ref[half, r2] = acc[j, r].astype(BF16)
                continue
            got = (acc[j, r], column(mlcol, at), column(mlcol, at + 1))
            got = joined(got, (merge[0][r2], column(mlin.at[2], at % 8), column(mlin.at[2], at % 8 + 1)))
            keep(mlcol, at, got[1], got[2])
            sums_ref[half, r2] = got[0].astype(BF16)
        ml_ref[half] = mlcol[...].T[j * 8 : j * 8 + 8]

    add_late(0)
    second_send(0, 0, t_opp, e_opp)
    put(12, t_opp.at[0], w_opp0, up_v)
    put(13, e_opp.at[0], f_opp0, up_v)
    second_send(0, 1, t_opp, e_opp)
    put(14, t_opp.at[1], w_opp1, dn_v)
    put(15, e_opp.at[1], f_opp1, dn_v)
    add_late(1)
    second_send(1, 1, t_up, e_up)
    put(16, t_up.at[1], w_up.at[1], up_v)
    put(17, e_up.at[1], f_up.at[1], up_v)
    add_late(2)
    second_send(2, 0, t_dn, e_dn)
    put(20, t_dn.at[0], w_dn.at[0], dn_v)
    put(21, e_dn.at[0], f_dn.at[0], dn_v)
    get(12, w_opp0)
    get(13, f_opp0)
    second_send(1, 0, t_up, e_up, (w_opp0, f_opp0))
    put(18, t_up.at[0], w_up.at[0], up_v)
    put(19, e_up.at[0], f_up.at[0], up_v)
    get(14, w_opp1)
    get(15, f_opp1)
    second_send(2, 1, t_dn, e_dn, (w_opp1, f_opp1))
    put(22, t_dn.at[1], w_dn.at[1], dn_v)
    put(23, e_dn.at[1], f_dn.at[1], dn_v)
    add_late(3)

    for half in (1, 0):
        get(16 if half else 18, w_up.at[half])
        get(17 if half else 19, f_up.at[half])
        get(22 if half else 20, w_dn.at[half])
        get(23 if half else 21, f_dn.at[half])
        flip_in(half * 2, f_up.at[half])
        flip_in(half * 2 + 1, f_dn.at[half])
    for r in range(4):
        half, r2 = r // 2, r % 2
        at = 24 + r * 2
        got = (acc[3, r], column(mlcol, at), column(mlcol, at + 1))
        for slot, ref in ((half * 2, w_up), (half * 2 + 1, w_dn)):
            got = joined(got, (ref[half, r2], column(mlin.at[slot], r * 2), column(mlin.at[slot], r * 2 + 1)))
        out_ref[r] = (got[0] / got[2]).astype(BF16)
    for copy in sent:
        copy.wait_send()


def vmem():
    return pl.BlockSpec(memory_space=pltpu.VMEM)


def anywhere():
    return pl.BlockSpec(memory_space=pl.ANY)


def body(latent_cache, index_keys, query_latent, index_query, index_gates, selected):
    rows, heads, width = query_latent.shape
    tokens = latent_cache.shape[0]
    kt = latent_cache.T
    q_latent = query_latent[:, :, :LATENT].transpose(1, 0, 2).reshape(heads, rows * LATENT)
    q_rope = query_latent[:, :, LATENT:].transpose(1, 0, 2).reshape(heads, rows * (width - LATENT))
    qw = jnp.concatenate([q_latent, q_rope], axis=1)
    gates = jnp.pad(index_gates.T, ((0, 0), (0, 128 - rows)))
    iqg = jnp.concatenate([index_query.reshape(-1, 128), gates], axis=0)
    dma = pltpu.SemaphoreType.DMA

    half = (4, 2, heads, LATENT)
    quarter = (2, heads, LATENT)
    _, index_scores, attended = pl.pallas_call(
        kernel,
        out_shape=(
            jax.ShapeDtypeStruct((16,) + qw.shape, BF16),
            jax.ShapeDtypeStruct((rows * 32, index_keys.shape[0]), F32),
            jax.ShapeDtypeStruct((rows, heads, LATENT), BF16),
        ),
        in_specs=[vmem(), vmem(), vmem(), anywhere(), vmem()],
        out_specs=(anywhere(), vmem(), vmem()),
        scratch_shapes=[
            pltpu.VMEM((8, 640, tokens), BF16),
            pltpu.VMEM((16, 16, 128), BF16),
            pltpu.VMEM((16, 2) + iqg.shape, BF16),
            pltpu.VMEM((16, 16, 128), BF16),
            pltpu.VMEM((512, 128), F32),
            pltpu.VMEM(index_keys.shape, BF16),
            pltpu.VMEM((2, 512, 512), F32),
            dma((20,)), dma((20,)), dma((20,)), dma((20,)), dma((21,)), dma((21,)),
            dma((9,)), dma((9,)), dma((16,)), dma((16,)), dma((5,)),
            pltpu.VMEM((16, 512, 640), BF16),
            pltpu.VMEM((2, 16, 144, 640), BF16),
            pltpu.VMEM((2, 4, heads, 256), BF16),
            pltpu.VMEM((2, 144, 512), F32),
            pltpu.VMEM((256, 128), F32),
            pltpu.VMEM((128, 128), F32),
            pltpu.VMEM((4, 128, 128), F32),
        ]
        + [pltpu.VMEM((2,) + half, BF16)] * 3
        + [pltpu.VMEM(half, BF16)] * 2
        + [pltpu.VMEM((2,) + half, BF16)] * 2
        + [pltpu.VMEM((2, 16, 128), F32)] * 3
        + [pltpu.VMEM((16, 128), F32)] * 2
        + [pltpu.VMEM((2, 16, 128), F32)] * 2
        + [pltpu.VMEM((4, rows, heads, LATENT), F32)]
        + [pltpu.VMEM((2,) + quarter, BF16)] * 3
        + [pltpu.VMEM(quarter, BF16)] * 2
        + [pltpu.VMEM((2,) + quarter, BF16)] * 2
        + [pltpu.VMEM((2, 8, 128), F32)] * 3
        + [pltpu.VMEM((8, 128), F32)] * 2
        + [pltpu.VMEM((2, 8, 128), F32)] * 2
        + [dma((2, 24)), dma((24,)), dma((24,))],
        compiler_params=pltpu.CompilerParams(
            collective_id=0, has_side_effects=True, vmem_limit_bytes=63 * 1024 * 1024
        ),
        name="attend",
    )(qw, kt, iqg, index_keys, selected)
    return attended, index_scores


def solution(mesh):
    return jax.shard_map(
        body,
        mesh=mesh,
        in_specs=(
            P(("ctx", "row"), None),
            P("ctx", None),
            P(("row", "ctx"), None, None),
            P(("row", "ctx"), None, None),
            P(("row", "ctx"), None),
            P(("row", "ctx"), None),
        ),
        out_specs=(P(("row", "ctx"), None, None), P("row", "ctx")),
        check_vma=False,
    )
```

```python
import math

import jax
import jax.numpy as jnp
from jax import lax
from jax.experimental import pallas as pl
from jax.experimental.pallas import tpu as pltpu
from jax.sharding import PartitionSpec as P

MESH = pl.DeviceIdType.MESH
LATENT = 512
TO_LOG2 = 192 ** (-0.5) * math.log2(math.e)
NONE = -1e30
FLOOR = -1e29
F32 = jnp.float32
BF16 = jnp.bfloat16
NT = (((1,), (1,)), ((), ()))


def remote(src, dst, send, recv, device):
    return pltpu.make_async_remote_copy(
        src_ref=src, dst_ref=dst, send_sem=send, recv_sem=recv, device_id=device, device_id_type=MESH
    )


def place(core):
    chip = lax.axis_index("ctx") // 2
    x, y = chip // 4, chip % 4
    return x * (1 - core) + y * core, y * (1 - core) + x * core


def chip_of(a, b, core):
    a, b = a % 4, b % 4
    return (a * (1 - core) + b * core) * 4 + b * (1 - core) + a * core


class Ring:
    def __init__(self, own, buf, rows, send, recv, core, on_block=None):
        self.own, self.buf, self.send, self.recv, self.core = own, buf, send, recv, core
        self.halves = (pl.ds(0, rows), pl.ds(0, rows // 2), pl.ds(rows // 2, rows // 2))
        self.a, self.b = place(core)
        self.columns = (self.a, self.a + 3, self.a + 1, self.a + 2)
        self.sent = []
        self.on_block = on_block

    def view(self, a, b, part):
        return self.buf(chip_of(a, b, self.core), self.halves[part])

    def put(self, k, block, part, to, own=False):
        src = self.own if own else self.view(*block, part)
        device = {"ctx": chip_of(*to, self.core) * 2 + self.core}
        copy = remote(src, self.view(*block, part), self.send.at[k], self.recv.at[k], device)
        copy.start()
        self.sent.append(copy)

    def get(self, k, block, part, event):
        ref = self.view(*block, part)
        remote(ref, ref, self.send.at[k], self.recv.at[k], {"ctx": lax.axis_index("ctx")}).wait_recv()
        if self.on_block is not None:
            self.on_block(event, block, part)

    def start(self):
        a, b = self.a, self.b
        self.put(4, (a, b), 0, (a, b + 1), own=True)
        self.put(5, (a, b), 0, (a, b + 3), own=True)
        self.put(0, (a, b), 0, (a + 1, b), own=True)
        self.put(1, (a, b), 0, (a + 3, b), own=True)

    def second(self, j):
        block = (self.columns[j], self.b)
        self.put(4 + 4 * j, block, 0, (self.a, self.b + 1))
        self.put(5 + 4 * j, block, 0, (self.a, self.b + 3))

    def near(self):
        a, b = self.a, self.b
        self.get(0, (a + 3, b), 0, 1)
        self.put(2, (a + 3, b), 1, (a + 1, b))
        self.second(1)
        self.get(1, (a + 1, b), 0, 2)
        self.put(3, (a + 1, b), 2, (a + 3, b))
        self.second(2)

    def far(self):
        a, b = self.a, self.b
        self.get(2, (a + 2, b), 1, 3)
        self.get(3, (a + 2, b), 2, 4)
        self.second(3)

    def relay(self, j):
        column, b = self.columns[j], self.b
        self.get(4 + 4 * j, (column, b + 3), 0, 5 + 4 * j)
        self.put(6 + 4 * j, (column, b + 3), 1, (self.a, b + 1))
        self.get(5 + 4 * j, (column, b + 1), 0, 6 + 4 * j)
        self.put(7 + 4 * j, (column, b + 1), 2, (self.a, b + 3))

    def last(self, j):
        column, b = self.columns[j], self.b
        self.get(6 + 4 * j, (column, b + 2), 1, 7 + 4 * j)
        self.get(7 + 4 * j, (column, b + 2), 2, 8 + 4 * j)

    def finish(self):
        for copy in self.sent:
            copy.wait_send()


def kernel(
    q_ref, k_ref, iq_ref, keys_hbm, sel_ref,
    qall, isc_ref, out_ref,
    kext, tall, iqall, tsend, gate_ref, keys_ref, logit_ref,
    q_send, q_recv, i_send, i_recv, p_send, p_recv, k_send, k_recv, t_send, t_recv, local,
    *attend_refs,
):
    ctx, z = lax.axis_index("ctx"), lax.axis_index("row")
    core, chip = ctx % 2, ctx // 2
    other = 1 - core
    partner = {"ctx": chip * 2 + other}
    x, y = chip // 4, chip % 4

    keys_copy = pltpu.make_async_copy(keys_hbm, keys_ref, local.at[4])
    keys_copy.start()
    ones = jnp.where(lax.broadcasted_iota(jnp.int32, (64, 1024), 0) == 0, 1.0, 0.0).astype(BF16)

    def set_ones(block, carry):
        kext[block, pl.ds(576, 64), :] = ones
        return carry

    lax.fori_loop(0, 8, set_ones, 0)
    barrier = pltpu.get_barrier_semaphore()
    for step in range(1, 16):
        pl.semaphore_signal(
            barrier, inc=1, device_id={"ctx": ((chip + step) % 16) * 2 + core}, device_id_type=MESH
        )
    pl.semaphore_signal(barrier, inc=1, device_id=partner, device_id_type=MESH)
    for step in (1, 3):
        pl.semaphore_signal(barrier, inc=1, device_id={"row": (z + step) % 4}, device_id_type=MESH)
    pl.semaphore_wait(barrier, 18)

    to_partner = []

    def hand_on(event, block, part):
        ref = index_ring.view(*block, part)
        copy = remote(ref, ref, p_send.at[event], p_recv.at[event], partner)
        copy.start()
        to_partner.append(copy)

    index_ring = Ring(
        iq_ref, lambda p, rows: iqall.at[p, core, rows], iq_ref.shape[0], i_send, i_recv, core, hand_on
    )
    index_ring.start()
    copy = remote(iq_ref, iqall.at[chip, core], p_send.at[0], p_recv.at[0], partner)
    copy.start()
    to_partner.append(copy)

    k_rows = k_ref.shape[0]
    parts = (pl.ds(0, k_rows), pl.ds(0, k_rows // 2), pl.ds(k_rows // 2, k_rows // 2))
    k_sent = []

    def k_view(depth, part, c=core):
        return kext.at[c * 4 + depth % 4, parts[part]]

    def k_put(k, src, dst, device):
        copy = remote(src, dst, k_send.at[k], k_recv.at[k], device)
        copy.start()
        k_sent.append(copy)

    def k_get(k, depth, part, c=core):
        ref = k_view(depth, part, c)
        remote(ref, ref, k_send.at[k], k_recv.at[k], {"row": z}).wait_recv()

    up, down = {"row": (z + 1) % 4}, {"row": (z + 3) % 4}
    query_ring = Ring(q_ref, lambda p, rows: qall.at[p, rows], q_ref.shape[0], q_send, q_recv, core)
    query_ring.start()
    k_put(0, k_ref, k_view(z, 0), up)
    k_put(1, k_ref, k_view(z, 0), down)
    k_put(4, k_ref, k_view(z, 0), partner)

    own = [
        pltpu.make_async_copy(iq_ref, iqall.at[chip, core], local.at[3]),
        pltpu.make_async_copy(q_ref, qall.at[chip], local.at[0]),
        pltpu.make_async_copy(k_ref, k_view(z, 0), local.at[1]),
    ]
    for copy in own:
        copy.start()

    pieces = sel_ref.shape[1] // 512

    def add_picks(i, total):
        at = pl.ds(pl.multiple_of((i % pieces) * 512, 512), 512)
        token = sel_ref[pl.ds(i // pieces, 1), at]
        to = (token >> 13) * 16 + ((token >> 4) & 15)
        window = (i // pieces) * 32 + ((token >> 8) & 31)
        value = ((token & 255) + 1).astype(F32)
        left = lax.broadcasted_iota(jnp.int32, (256, 512), 0) == to
        right = lax.broadcasted_iota(jnp.int32, (128, 512), 0) == window
        return total + lax.dot_general(
            jnp.where(left, 1.0, 0.0).astype(BF16),
            jnp.where(right, value, 0.0).astype(BF16),
            NT,
            preferred_element_type=F32,
        )

    table = lax.fori_loop(0, sel_ref.shape[0] * pieces, add_picks, jnp.zeros((256, 128), F32))
    tsend[...] = table.astype(BF16).reshape(16, 16, 128)

    table_copies = []

    def send_tables():
        for step in range(1, 16):
            to = (chip + step) % 16
            copy = remote(
                tsend.at[to], tall.at[chip], t_send.at[step], t_recv.at[step], {"ctx": to * 2 + core}
            )
            copy.start()
            table_copies.append(copy)
        own.append(pltpu.make_async_copy(tsend.at[chip], tall.at[chip], local.at[2]))
        own[-1].start()

    oa, ob = place(other)
    columns = (0, 3, 1, 2)

    def wait_partner(da, db):
        if db:
            j = columns.index(da)
            events = {3: ((5 + 4 * j, 0),), 1: ((6 + 4 * j, 0),), 2: ((7 + 4 * j, 1), (8 + 4 * j, 2))}[db]
        else:
            events = {0: ((0, 0),), 3: ((1, 0),), 1: ((2, 0),), 2: ((3, 1), (4, 2))}[da]
        for event, part in events:
            ref = iqall.at[chip_of(oa + da, ob + db, other), other, index_ring.halves[part]]
            remote(ref, ref, p_send.at[event], p_recv.at[event], partner).wait_recv()

    tile = 512
    tiles = keys_ref.shape[0] // tile

    def index_chip(p):
        for c in range(2):
            gates = iqall[p, c, 256:320, :].astype(F32)
            for r in range(4):
                gate_ref[pl.ds((c * 4 + r) * 64, 64), :] = jnp.broadcast_to(gates[:, r : r + 1], (64, 128))

        def token_tile(t):
            return pl.ds(pl.multiple_of(t * tile, tile), tile)

        def logits(t, slot):
            logit_ref[slot] = lax.dot_general(
                iqall[p, :, 0:256, :].reshape(512, 128), keys_ref[token_tile(t), :], NT, preferred_element_type=F32
            )

        def gated_sum(t, slot):
            columns = []
            for lanes in range(0, tile, 128):
                rows = []
                for i in range(8):
                    total = None
                    for h in range(0, 64, 8):
                        part = logit_ref[slot, i * 64 + h : i * 64 + h + 8, lanes : lanes + 128]
                        part = jnp.maximum(part, 0.0) * gate_ref[i * 64 + h : i * 64 + h + 8, :]
                        total = part if total is None else total + part
                    rows.append(jnp.sum(total, axis=0, keepdims=True))
                columns.append(jnp.concatenate(rows, axis=0))
            isc_ref[pl.ds(pl.multiple_of(p * 8, 8), 8), token_tile(t)] = jnp.concatenate(columns, axis=1)

        logits(0, 0)

        def two_tiles(i, carry):
            logits(i * 2 + 1, 1)
            gated_sum(i * 2, 0)
            logits(jnp.minimum(i * 2 + 2, tiles - 1), 0)
            gated_sum(i * 2 + 1, 1)
            return carry

        lax.fori_loop(0, tiles // 2, two_tiles, 0)

    def index_chips(low, high, dx, dy):
        def one(k, carry):
            index_chip((x + dx(k)) % 4 * 4 + (y + dy(k)) % 4)
            return carry

        lax.fori_loop(low, high, one, 0)

    beside = (lambda k: (1 - k // 2) * (1 + 2 * (k % 2)), lambda k: (k // 2) * (1 + 2 * (k % 2)))
    corner = (lambda k: 1 + 2 * (k % 2), lambda k: 1 + 2 * (k // 2))
    rest = (
        lambda k: 2 * (k == 0) + 2 * (k == 2) + 2 * (k == 3) + (k == 4) + 3 * (k == 5) + 2 * (k == 6),
        lambda k: 2 * (k == 1) + (k == 2) + 3 * (k == 3) + 2 * (k == 4) + 2 * (k == 5) + 2 * (k == 6),
    )

    index_ring.near()
    send_tables()
    index_ring.relay(0)
    own[0].wait()
    keys_copy.wait()
    wait_partner(0, 0)
    index_chips(0, 1, lambda k: k, lambda k: k)
    index_ring.far()
    index_ring.relay(1)
    index_ring.relay(2)
    index_ring.last(0)
    index_ring.relay(3)
    for j in (1, 2, 3):
        index_ring.last(j)
    query_ring.near()
    query_ring.relay(0)
    for da, db in ((3, 0), (1, 0), (0, 3), (0, 1)):
        wait_partner(da, db)
    index_chips(0, 4, *beside)
    query_ring.far()
    k_get(0, z + 3, 0)
    k_put(2, k_view(z + 3, 1), k_view(z + 3, 1), up)
    k_put(5, k_view(z + 3, 0), k_view(z + 3, 0), partner)
    k_get(1, z + 1, 0)
    k_put(3, k_view(z + 1, 2), k_view(z + 1, 2), down)
    k_put(6, k_view(z + 1, 0), k_view(z + 1, 0), partner)
    for da, db in ((3, 3), (3, 1), (1, 3), (1, 1)):
        wait_partner(da, db)
    index_chips(0, 2, *corner)
    query_ring.relay(1)
    query_ring.relay(2)
    index_chips(2, 4, *corner)
    for da, db in ((2, 0), (0, 2), (3, 2), (1, 2), (2, 3), (2, 1), (2, 2)):
        wait_partner(da, db)
    index_chips(0, 3, *rest)
    query_ring.relay(3)
    k_get(2, z + 2, 1)
    k_put(7, k_view(z + 2, 1), k_view(z + 2, 1), partner)
    k_get(3, z + 2, 2)
    k_put(8, k_view(z + 2, 2), k_view(z + 2, 2), partner)
    index_chips(3, 7, *rest)

    k_get(4, z, 0, other)
    k_get(5, z + 3, 0, other)
    k_get(6, z + 1, 0, other)
    k_get(7, z + 2, 1, other)
    k_get(8, z + 2, 2, other)
    for step in range(1, 16):
        frm = (chip + 16 - step) % 16
        remote(
            tall.at[frm], tall.at[frm], t_send.at[step], t_recv.at[step], partner
        ).wait_recv()
    for copy in own[1:]:
        copy.wait()

    def queries_here():
        for j in range(4):
            query_ring.last(j)

    attend(qall, kext, tall, out_ref, queries_here, *attend_refs)
    query_ring.finish()
    index_ring.finish()
    for copy in to_partner + table_copies + k_sent:
        copy.wait_send()


def attend(
    qall, kext, tall, out_ref, queries_here,
    ksel, qbuf, rope, raw, picks, mlcol, mlin,
    s_opp, s_up, s_dn, r_opp0, r_opp1, r_up, r_dn,
    m_opp, m_up, m_dn, n_opp0, n_opp1, n_up, n_dn,
    acc, t_opp, t_up, t_dn, w_opp0, w_opp1, w_up, w_dn,
    e_opp, e_up, e_dn, f_opp0, f_opp1, f_up, f_dn,
    q_sem, send, recv,
):
    ctx = lax.axis_index("ctx")
    core = ctx % 2
    u, v = place(core)
    up_u = {"ctx": chip_of(u + 1, v, core) * 2 + core}
    dn_u = {"ctx": chip_of(u + 3, v, core) * 2 + core}
    up_v = {"ctx": chip_of(u, v + 1, core) * 2 + core}
    dn_v = {"ctx": chip_of(u, v + 3, core) * 2 + core}
    order = (2, 1, 3, 0)

    groups = ((2, 2), (3, 1), (1, 3), (0, 0))

    def q_copies(group):
        copies = []
        for j in range(4):
            for half in range(2):
                chip = chip_of(u + groups[group][half], v + order[j], core)
                for r in (half * 2, half * 2 + 1):
                    copies.append((
                        qall.at[chip, :, pl.ds(r * 512, 512)],
                        qbuf.at[group % 2, j * 4 + r, pl.ds(0, 128), pl.ds(0, 512)],
                    ))
                copies.append((
                    qall.at[chip, :, pl.ds(2048 + half * 128, 128)],
                    rope.at[group % 2, j, :, pl.ds(half * 128, 128)],
                ))
        return [
            pltpu.make_async_copy(src, dst, q_sem.at[group % 2, n]) for n, (src, dst) in enumerate(copies)
        ]

    probe = jnp.where(lax.broadcasted_iota(jnp.int32, (16, 640), 1) == 576, 1.0, 0.0).astype(BF16)

    def set_probe(row, carry):
        for slot in range(2):
            qbuf[slot, row, pl.ds(128, 16), :] = probe
        return carry

    lax.fori_loop(0, 16, set_probe, 0)
    sent = []

    def put(k, src, dst, device):
        copy = remote(src, dst, send.at[k], recv.at[k], device)
        copy.start()
        sent.append(copy)

    def get(k, ref):
        remote(ref, ref, send.at[k], recv.at[k], up_u).wait_recv()

    lane = lax.broadcasted_iota(jnp.int32, (128, 128), 1)

    def column(ref, at):
        return jnp.sum(jnp.where(lane == at, ref[...], 0.0), axis=1, keepdims=True)

    def keep(ref, at, peak, total):
        ref[...] = jnp.where(lane == at, peak, jnp.where(lane == at + 1, total, ref[...]))

    def flip_in(slot, ref):
        rows = ref.shape[0]
        full = jnp.concatenate([ref[...], jnp.zeros((128 - rows, 128), F32)], axis=0)
        mlin[slot] = full.T

    def joined(one, two):
        sums1, peak1, total1 = one
        sums2, peak2, total2 = two
        peak = jnp.maximum(peak1, peak2)
        f1, f2 = jnp.exp2((peak1 - peak) * TO_LOG2), jnp.exp2((peak2 - peak) * TO_LOG2)
        return sums1 * f1 + sums2.astype(F32) * f2, peak, total1 * f1 + total2 * f2

    def gather_tokens(chunk):
        for j in range(4):
            for r in range(4):
                t = tall[chip_of(u + groups[chunk][r // 2], v + order[j], core)].astype(F32)
                moved = t if r == 0 else pltpu.roll(t, 128 - r * 32, axis=1)
                picks[pl.ds((j * 4 + r) * 16, 16), :] = moved
        wide = lax.broadcasted_iota(jnp.int32, (256, 128), 1)
        token = (lax.broadcasted_iota(jnp.int32, (256, 256), 1) + 1).astype(F32)

        def some_windows(i, carry):
            for step in range(4):
                w = i * 4 + step
                want = jnp.sum(jnp.where(wide == w, picks[...], 0.0), axis=1, keepdims=True)
                onehot = jnp.where(token == want, 1.0, 0.0).astype(BF16)
                rows = lax.dot_general(
                    onehot, kext[i, :, step * 256 : (step + 1) * 256], NT, preferred_element_type=F32
                )
                at = pl.ds(pl.multiple_of(w * 16, 16), 16)
                ksel[:, at, :] = rows.astype(BF16).reshape(16, 16, 640)
            return carry

        lax.fori_loop(0, 8, some_windows, 0)

    def set_rope(slot):
        def one_block(j, carry):
            for r in range(4):
                part = rope[slot, j, :, r * 64 : (r + 1) * 64]
                qbuf[slot, j * 4 + r, pl.ds(0, 128), pl.ds(512, 128)] = jnp.concatenate(
                    [part, jnp.zeros((128, 64), BF16)], axis=1
                )
            return carry

        lax.fori_loop(0, 4, one_block, 0)

    def score_row(slot, row, to):
        raw[to] = lax.dot_general(qbuf[slot, row], ksel[row], NT, preferred_element_type=F32)

    def attend_row(row, frm):
        scores = jnp.where(raw[frm, 128:129, :] > 0.5, raw[frm, 0:128, :], NONE)
        peak = jnp.maximum(jnp.max(scores, axis=1, keepdims=True), FLOOR)
        weights = jnp.exp2((scores - peak) * TO_LOG2)
        total = jnp.sum(weights, axis=1, keepdims=True)
        sums = jnp.dot(weights.astype(BF16), ksel[row, :, 0:512], preferred_element_type=F32)
        return sums, peak, total

    def half_chunk(chunk, half, put_row, merges):
        slot = chunk % 2
        score_row(slot, half * 2, 0)

        def one_block(j, carry):
            for r2 in range(2):
                row = j * 4 + half * 2 + r2
                score_row(slot, (row + 1 if r2 == 0 else jnp.minimum(row + 3, 12 + half * 2)), 1 - r2)
                got = attend_row(row, r2)
                for at_slot, ref in merges:
                    at = j * 4 + r2 * 2
                    got = joined(
                        got, (ref[j, r2], column(mlin.at[at_slot], at), column(mlin.at[at_slot], at + 1))
                    )
                put_row(j, r2, *got)
            return carry

        lax.fori_loop(0, 4, one_block, 0)

    def send_half(chunk, half, sums_ref, ml_ref, merges):
        def put_row(j, r2, sums, peak, total):
            sums_ref[half, j, r2] = sums.astype(BF16)
            keep(mlcol, j * 4 + r2 * 2, peak, total)

        half_chunk(chunk, half, put_row, merges)
        ml_ref[half] = mlcol[...].T[0:16]

    mlcol[...] = jnp.zeros((128, 128), F32)

    def next_chunk(chunk):
        if chunk == 0:
            gather_tokens(chunk)
            queries_here()
            for copy in q_copies(chunk):
                copy.start()
        for copy in q_copies(chunk):
            copy.wait()
        if chunk < 3:
            for copy in q_copies(chunk + 1):
                copy.start()
        set_rope(chunk % 2)
        if chunk:
            gather_tokens(chunk)

    next_chunk(0)
    send_half(0, 0, s_opp, m_opp, ())
    put(0, s_opp.at[0], r_opp0, up_u)
    put(1, m_opp.at[0], n_opp0, up_u)
    send_half(0, 1, s_opp, m_opp, ())
    put(2, s_opp.at[1], r_opp1, dn_u)
    put(3, m_opp.at[1], n_opp1, dn_u)

    next_chunk(1)
    send_half(1, 1, s_up, m_up, ())
    put(4, s_up.at[1], r_up.at[1], up_u)
    put(5, m_up.at[1], n_up.at[1], up_u)
    send_half(1, 0, s_dn, m_dn, ())
    put(8, s_dn.at[0], r_dn.at[0], dn_u)
    put(9, m_dn.at[0], n_dn.at[0], dn_u)

    next_chunk(2)
    get(0, r_opp0)
    get(1, n_opp0)
    flip_in(0, n_opp0)
    send_half(2, 0, s_up, m_up, ((0, r_opp0),))
    put(6, s_up.at[0], r_up.at[0], up_u)
    put(7, m_up.at[0], n_up.at[0], up_u)
    get(2, r_opp1)
    get(3, n_opp1)
    flip_in(0, n_opp1)
    send_half(2, 1, s_dn, m_dn, ((0, r_opp1),))
    put(10, s_dn.at[1], r_dn.at[1], dn_u)
    put(11, m_dn.at[1], n_dn.at[1], dn_u)

    next_chunk(3)
    for half, early, early_ml, k in ((0, r_dn, n_dn, 8), (1, r_up, n_up, 4)):
        get(k, early.at[half])
        get(k + 1, early_ml.at[half])
        flip_in(0, early_ml.at[half])

        def put_row(j, r2, sums, peak, total):
            acc[j, half * 2 + r2] = sums
            keep(mlcol, j * 8 + half * 4 + r2 * 2, peak, total)

        half_chunk(3, half, put_row, ((0, early.at[half]),))

    get(6, r_up.at[0])
    get(7, n_up.at[0])
    flip_in(0, n_up.at[0])
    get(10, r_dn.at[1])
    get(11, n_dn.at[1])
    flip_in(1, n_dn.at[1])

    def add_late(j):
        for r in range(4):
            half, r2 = r // 2, r % 2
            at, here = j * 4 + r2 * 2, j * 8 + r * 2
            late = (r_up, r_dn)[half][half, j, r2]
            got = (acc[j, r], column(mlcol, here), column(mlcol, here + 1))
            got = joined(got, (late, column(mlin.at[half], at), column(mlin.at[half], at + 1)))
            acc[j, r] = got[0]
            keep(mlcol, here, got[1], got[2])

    def second_send(j, half, sums_ref, ml_ref, merge=None):
        if merge is not None:
            flip_in(2, merge[1])
        for r2 in range(2):
            r = half * 2 + r2
            at = j * 8 + r * 2
            if merge is None:
                sums_ref[half, r2] = acc[j, r].astype(BF16)
                continue
            got = (acc[j, r], column(mlcol, at), column(mlcol, at + 1))
            got = joined(got, (merge[0][r2], column(mlin.at[2], at % 8), column(mlin.at[2], at % 8 + 1)))
            keep(mlcol, at, got[1], got[2])
            sums_ref[half, r2] = got[0].astype(BF16)
        ml_ref[half] = mlcol[...].T[j * 8 : j * 8 + 8]

    add_late(0)
    second_send(0, 0, t_opp, e_opp)
    put(12, t_opp.at[0], w_opp0, up_v)
    put(13, e_opp.at[0], f_opp0, up_v)
    second_send(0, 1, t_opp, e_opp)
    put(14, t_opp.at[1], w_opp1, dn_v)
    put(15, e_opp.at[1], f_opp1, dn_v)
    add_late(1)
    second_send(1, 1, t_up, e_up)
    put(16, t_up.at[1], w_up.at[1], up_v)
    put(17, e_up.at[1], f_up.at[1], up_v)
    add_late(2)
    second_send(2, 0, t_dn, e_dn)
    put(20, t_dn.at[0], w_dn.at[0], dn_v)
    put(21, e_dn.at[0], f_dn.at[0], dn_v)
    get(12, w_opp0)
    get(13, f_opp0)
    second_send(1, 0, t_up, e_up, (w_opp0, f_opp0))
    put(18, t_up.at[0], w_up.at[0], up_v)
    put(19, e_up.at[0], f_up.at[0], up_v)
    get(14, w_opp1)
    get(15, f_opp1)
    second_send(2, 1, t_dn, e_dn, (w_opp1, f_opp1))
    put(22, t_dn.at[1], w_dn.at[1], dn_v)
    put(23, e_dn.at[1], f_dn.at[1], dn_v)
    add_late(3)

    for half in (1, 0):
        get(16 if half else 18, w_up.at[half])
        get(17 if half else 19, f_up.at[half])
        get(22 if half else 20, w_dn.at[half])
        get(23 if half else 21, f_dn.at[half])
        flip_in(half * 2, f_up.at[half])
        flip_in(half * 2 + 1, f_dn.at[half])
    for r in range(4):
        half, r2 = r // 2, r % 2
        at = 24 + r * 2
        got = (acc[3, r], column(mlcol, at), column(mlcol, at + 1))
        for slot, ref in ((half * 2, w_up), (half * 2 + 1, w_dn)):
            got = joined(got, (ref[half, r2], column(mlin.at[slot], r * 2), column(mlin.at[slot], r * 2 + 1)))
        out_ref[r] = (got[0] / got[2]).astype(BF16)
    for copy in sent:
        copy.wait_send()


def vmem():
    return pl.BlockSpec(memory_space=pltpu.VMEM)


def anywhere():
    return pl.BlockSpec(memory_space=pl.ANY)


def body(latent_cache, index_keys, query_latent, index_query, index_gates, selected):
    rows, heads, width = query_latent.shape
    tokens = latent_cache.shape[0]
    kt = latent_cache.T
    q_latent = query_latent[:, :, :LATENT].transpose(1, 0, 2).reshape(heads, rows * LATENT)
    q_rope = query_latent[:, :, LATENT:].transpose(1, 0, 2).reshape(heads, rows * (width - LATENT))
    qw = jnp.concatenate([q_latent, q_rope], axis=1)
    gates = jnp.pad(index_gates.T, ((0, 0), (0, 128 - rows)))
    iqg = jnp.concatenate([index_query.reshape(-1, 128), gates], axis=0)
    dma = pltpu.SemaphoreType.DMA

    half = (4, 2, heads, LATENT)
    quarter = (2, heads, LATENT)
    _, index_scores, attended = pl.pallas_call(
        kernel,
        out_shape=(
            jax.ShapeDtypeStruct((16,) + qw.shape, BF16),
            jax.ShapeDtypeStruct((rows * 32, index_keys.shape[0]), F32),
            jax.ShapeDtypeStruct((rows, heads, LATENT), BF16),
        ),
        in_specs=[vmem(), vmem(), vmem(), anywhere(), vmem()],
        out_specs=(anywhere(), vmem(), vmem()),
        scratch_shapes=[
            pltpu.VMEM((8, 640, tokens), BF16),
            pltpu.VMEM((16, 16, 128), BF16),
            pltpu.VMEM((16, 2) + iqg.shape, BF16),
            pltpu.VMEM((16, 16, 128), BF16),
            pltpu.VMEM((512, 128), F32),
            pltpu.VMEM(index_keys.shape, BF16),
            pltpu.VMEM((2, 512, 512), F32),
            dma((20,)), dma((20,)), dma((20,)), dma((20,)), dma((21,)), dma((21,)),
            dma((9,)), dma((9,)), dma((16,)), dma((16,)), dma((5,)),
            pltpu.VMEM((16, 512, 640), BF16),
            pltpu.VMEM((2, 16, 144, 640), BF16),
            pltpu.VMEM((2, 4, heads, 256), BF16),
            pltpu.VMEM((2, 144, 512), F32),
            pltpu.VMEM((256, 128), F32),
            pltpu.VMEM((128, 128), F32),
            pltpu.VMEM((4, 128, 128), F32),
        ]
        + [pltpu.VMEM((2,) + half, BF16)] * 3
        + [pltpu.VMEM(half, BF16)] * 2
        + [pltpu.VMEM((2,) + half, BF16)] * 2
        + [pltpu.VMEM((2, 16, 128), F32)] * 3
        + [pltpu.VMEM((16, 128), F32)] * 2
        + [pltpu.VMEM((2, 16, 128), F32)] * 2
        + [pltpu.VMEM((4, rows, heads, LATENT), F32)]
        + [pltpu.VMEM((2,) + quarter, BF16)] * 3
        + [pltpu.VMEM(quarter, BF16)] * 2
        + [pltpu.VMEM((2,) + quarter, BF16)] * 2
        + [pltpu.VMEM((2, 8, 128), F32)] * 3
        + [pltpu.VMEM((8, 128), F32)] * 2
        + [pltpu.VMEM((2, 8, 128), F32)] * 2
        + [dma((2, 24)), dma((24,)), dma((24,))],
        compiler_params=pltpu.CompilerParams(
            collective_id=0, has_side_effects=True, vmem_limit_bytes=63 * 1024 * 1024
        ),
        name="attend",
    )(qw, kt, iqg, index_keys, selected)
    return attended, index_scores


def solution(mesh):
    return jax.shard_map(
        body,
        mesh=mesh,
        in_specs=(
            P(("ctx", "row"), None),
            P("ctx", None),
            P(("row", "ctx"), None, None),
            P(("row", "ctx"), None, None),
            P(("row", "ctx"), None),
            P(("row", "ctx"), None),
        ),
        out_specs=(P(("row", "ctx"), None, None), P("row", "ctx")),
        check_vma=False,
    )
```
